512 devices in a mesh: row: 32 (over x, y), rhs: 16 (over z, core).
Axes of the slice: x: 4, y: 8, z: 8, core: 2. Of those that a mesh axis runs over, the one named last changes fastest.
Arguments:
- factor: float32 [32, 704, 4, 1024], P('row', None, None, 'rhs'), may hold values from -0.09375 to 0.09375
- inverses: float32 [32, 4, 1024, 32], P('row', None, 'rhs'), may hold values from -0.1875 to 0.1875
- right_side: float32 [32, 704, 4096], P('row', None, 'rhs'), may hold values from -6 to 6
Outputs:
- solution: float32 [32, 128, 4096], P('row', None, 'rhs')
- trailing: float32 [32, 576, 4096], P('row', None, 'rhs')
The draws below stay inside these ranges and needn't reach their ends.
All inputs are finite; a program needn't handle non-finite values.
Results may differ from the reference program's by a relative error of at most 0.0001.
Values sent between devices are 32-bit elements; how exact they have to be, the bound alone decides.
No kernel may reach another device: no remote copies, remote signals or barrier semaphores. Data moves between devices by JAX's collectives and lax.ppermute only.
A program may use at most 64 MiB of HBM per device.

```python
import jax
import jax.numpy as jnp
from jax import lax

PB = 1024
PANELS = 4
NRHS = 4096
PD = 32
ROWS_DEV = 704
N_ROW = 32


def level_of(stream_key, dims, cuts, least, top_value):
    loudness = 1.0
    for axis_at, shards_of in cuts:
        heights = jax.random.uniform(jax.random.fold_in(jax.random.fold_in(stream_key, 6), axis_at), (shards_of,), jnp.float32, least / len(cuts), top_value / len(cuts))
        loudness = loudness * jnp.repeat(jnp.exp(heights), dims[axis_at] // shards_of).reshape((-1,) + (1,) * (len(dims) - 1 - axis_at))
    return loudness


def scatter_about(stream_key, dims, width, reach, shards=(), held_as=jnp.bfloat16):
    drawn = width * jax.random.normal(stream_key, dims, jnp.float32)
    if shards:
        drawn = drawn * level_of(stream_key, dims, shards, -0.22, 0.18)
    return jnp.clip(drawn, -reach, reach).astype(held_as)


def setup_inputs(seed: int = 0) -> dict:
    keys = jax.random.split(jax.random.key(seed), 4)
    factor = scatter_about(keys[0], (N_ROW, ROWS_DEV, PANELS, PB), (PANELS * PB) ** -0.5, 0.09375, ((0, 32), (3, 16)), jnp.float32)
    inverses = scatter_about(keys[1], (N_ROW, PANELS, PB, PD), PB ** -0.5, 0.1875, ((0, 32), (2, 16)), jnp.float32)
    right_side = scatter_about(keys[2], (N_ROW, ROWS_DEV, NRHS), 1.0, 6.0, ((0, 32), (2, 16)), jnp.float32)
    return dict(factor=factor, inverses=inverses, right_side=right_side)


def reference(factor, inverses, right_side):
    current = right_side
    pieces = []
    for k in range(PANELS):
        low = k * PD
        high = (k + 1) * PD
        block = current[:, low:high, :].reshape(PB, NRHS)
        diagonal = jnp.transpose(inverses[:, k], (1, 0, 2)).reshape(PB, PB)
        solved = jnp.dot(diagonal, block, precision=lax.Precision.HIGHEST, preferred_element_type=jnp.float32)
        pieces.append(solved.reshape(N_ROW, PD, NRHS))
        change = jnp.einsum("rjc,cd->rjd", factor[:, high:, k, :], solved, precision=lax.Precision.HIGHEST)
        current = current.at[:, high:, :].add(-change)
    solution = jnp.concatenate(pieces, axis=1)
    trailing = current[:, PANELS * PD:, :]
    return solution, trailing
```

```python
import jax
import jax.numpy as jnp
from jax import lax
from jax.sharding import Mesh, PartitionSpec as P

PREC = lax.Precision.HIGH
QUADS = 4
RHS = ("z", "core")
GROUP = ("x", "yp")


def spread(array, axes):
    length = lax.axis_size(axes)
    return lax.all_to_all(
        jnp.broadcast_to(array[None], (length, *array.shape)), axes, 0, 0, tiled=True
    )


def body(factor, inverses, right_side):
    lower = jnp.transpose(factor[0], (1, 2, 0))
    inv = inverses[0]
    current = right_side[0]
    panels, cols, _ = lower.shape
    width = inv.shape[2]
    count = current.shape[1]
    tail = panels * width
    quads = lax.axis_size("yq")
    nx, npair = lax.axis_size("x"), lax.axis_size("yp")
    group = nx * npair
    per = count // quads
    rows = quads * width
    half = cols // npair

    small = jnp.concatenate(
        [lower[k, :, (k + 1) * width : tail] for k in range(panels - 1)], axis=1
    )
    steps = small.shape[1] // width
    diag = jnp.transpose(inv, (1, 0, 2)).reshape(cols, panels * width)
    shared = jnp.concatenate([small, diag], axis=1)
    first = jnp.transpose(current[:tail]).reshape(quads, per, tail)
    sent = jnp.concatenate(
        [first, jnp.broadcast_to(shared[None], (quads, *shared.shape))], axis=2
    )
    got = lax.all_to_all(sent, "yq", 0, 0, tiled=True)
    heads = jnp.transpose(
        got[:, :, :tail].reshape(quads, per, panels, width), (2, 1, 0, 3)
    ).reshape(panels, per, rows)
    small = jnp.transpose(
        got[:, :, tail : tail + steps * width].reshape(quads, cols, steps, width), (1, 2, 0, 3)
    ).reshape(cols, steps * rows)
    diag = jnp.transpose(
        got[:, :, tail + steps * width :].reshape(quads, cols, panels, width), (1, 2, 0, 3)
    ).reshape(cols, panels * rows)

    diag0 = spread(diag[:, :rows], RHS)
    rest = jnp.concatenate([diag[:, rows:], small], axis=1)
    rest = lax.all_gather(rest.reshape(npair, half, -1), RHS, axis=1)
    trail = jnp.transpose(lower[:, :, tail:], (1, 0, 2)).reshape(npair, half, -1)
    trail, _ = lax.optimization_barrier((trail, rest[0, 0, 0, 0]))
    trail = lax.all_gather(trail, RHS, axis=1)

    def by_group(block):
        return block.reshape(npair, nx, rows, block.shape[-1])

    def diagonal(k):
        if k == 0:
            return jnp.transpose(
                diag0.reshape(nx, quads, npair, half, rows), (2, 0, 1, 3, 4)
            ).reshape(npair, nx, rows, rows)
        return by_group(rest[..., (k - 1) * rows : k * rows])

    offset = (panels - 1) * rows
    whole = []
    for k in range(panels):
        partial = jnp.einsum(
            "mj,pxij->xpmi", heads[k], diagonal(k), precision=PREC,
            preferred_element_type=jnp.float32,
        ).reshape(group, per, rows)
        mine = lax.all_to_all(partial, GROUP, 0, 0, tiled=True).sum(axis=0)
        if k < panels - 1:
            solved = spread(mine, GROUP)
            n = (panels - 1 - k) * rows
            lines = by_group(rest[..., offset : offset + n])
            offset += n
            change = jnp.einsum(
                "xpmc,pxcn->mn", solved.reshape(nx, npair, per, rows), lines,
                precision=PREC, preferred_element_type=jnp.float32,
            )
            update = jnp.transpose(change.reshape(per, panels - 1 - k, rows), (1, 0, 2))
            heads = heads.at[k + 1 :].add(-update)
            every = spread(solved, "yq")
            every = jnp.transpose(every, (1, 0, 2, 3))
        else:
            every = spread(spread(mine, "yq"), GROUP)
        whole.append(every.reshape(nx, npair, count, rows))

    place = lax.axis_index("x") * npair + lax.axis_index("yp")
    lane = lax.axis_index("yq") * width
    mine = []
    total = 0
    for k in range(panels):
        got = whole[k].reshape(group, count, rows)
        piece = lax.dynamic_slice(got, (place, 0, lane), (1, count, width))[0]
        mine.append(jnp.transpose(piece))
        width_tail = lower.shape[2] - tail
        lines = by_group(trail[..., k * width_tail : (k + 1) * width_tail])
        total = total + jnp.einsum(
            "xpmc,pxcn->nm", whole[k], lines, precision=PREC,
            preferred_element_type=jnp.float32,
        )
    return (jnp.concatenate(mine, axis=0)[None], (current[tail:] - total)[None])


def solution(mesh):
    nx, ny, nz, nc = SIZES(mesh)
    fine = Mesh(
        mesh.devices.reshape(nx, QUADS, ny // QUADS, nz, nc), ("x", "yq", "yp", "z", "core")
    )
    row = ("x", "yq", "yp")
    in_specs = (P(row, None, None, RHS), P(row, None, RHS, None), P(row, None, RHS))
    out_specs = (P(row, None, RHS), P(row, None, RHS))
    return jax.shard_map(body, mesh=fine, in_specs=in_specs, out_specs=out_specs, check_vma=False)


def SIZES(mesh):
    nrow, nrhs = mesh.shape["row"], mesh.shape["rhs"]
    nx = 4 if nrow % 32 == 0 else 2
    return nx, nrow // nx, nrhs // 2, 2
```

```python
import jax
import jax.numpy as jnp
from jax import lax
from jax.experimental import pallas as pl
from jax.experimental.pallas import tpu as pltpu
from jax.sharding import Mesh, PartitionSpec as P

QUADS = 4
RHS = ("z", "core")
GROUP = ("yp", "x")
F32 = jnp.float32


def halves(value):
    high = value.astype(jnp.bfloat16)
    return high, (value - high.astype(F32)).astype(jnp.bfloat16)


def dot(a, b, dims):
    def one(u, v):
        return lax.dot_general(u, v, (dims, ((), ())), preferred_element_type=F32)

    ah, al = halves(a)
    bh, bl = halves(b)
    return one(ah, bh) + (one(ah, bl) + one(al, bh))


NN = ((1,), (0,))
NT = ((1,), (1,))


def call(kernel, shapes, in_specs=None, **more):
    shapes = [jax.ShapeDtypeStruct(s, F32) for s in shapes]
    out = pl.pallas_call(
        kernel,
        out_shape=shapes,
        grid=(1,),
        in_specs=in_specs,
        **more,
    )
    return out


def whole(shape):
    return pl.BlockSpec(shape, lambda i: (0,) * len(shape))


def pack(f_ref, inv_ref, r_ref, out_ref):
    quads, _, _ = out_ref.shape
    cols = f_ref.shape[1]
    per = r_ref.shape[1] // quads
    w = inv_ref.shape[1]
    turned = r_ref[...].T
    wide = jnp.concatenate([f_ref[0][:, w:], f_ref[2][:, 3 * w :]], axis=1)
    mid = f_ref[1][:, 2 * w :]
    mid = jnp.concatenate([mid[: cols // 2], mid[cols // 2 :]], axis=1)
    diag = jnp.concatenate([inv_ref[k].T for k in range(4)], axis=1)
    for q in range(quads):
        out_ref[q, :per] = turned[q * per : (q + 1) * per]
        out_ref[q, per : per + cols] = wide
        out_ref[q, per + cols : per + cols + cols // 2] = mid
        out_ref[q, per + cols + cols // 2 :] = diag


def sort(w, per, got_ref, heads_ref, pay_ref, first_ref):
    quads = got_ref.shape[0]
    half = pay_ref.shape[2]
    cols = 2 * half
    a, b, d = per, per + cols, per + cols + half

    def lanes(start, n, at):
        return jnp.concatenate(
            [got_ref[q, start : start + n][:, at : at + w] for q in range(quads)], axis=1
        )

    for k in range(4):
        heads_ref[k] = lanes(0, per, k * w)
    for h in range(2):
        for k in range(1, 4):
            pay_ref[k - 1, h] = lanes(d + h * half, half, k * w)
        for j in range(3):
            pay_ref[3 + j, h] = lanes(a + h * half, half, j * w)
        for j in range(2):
            pay_ref[6 + j, h] = lanes(b, half, h * 2 * w + j * w)
        pay_ref[8, h] = lanes(a + h * half, half, 3 * w)
        piece = lanes(d + h * half, half, 0)
        for c in range(first_ref.shape[0]):
            first_ref[c, h] = piece


def begin(head_ref, first_ref, out_ref):
    blocks, pair, half, rows = first_ref.shape
    head = head_ref[0]
    for p in range(pair):
        block = first_ref[:, p].reshape(blocks * half, rows)
        y = dot(head, block, NT)
        n = blocks * half // rows
        for x in range(n):
            out_ref[p * n + x] = y[:, x * rows : (x + 1) * rows]


def add_up(got_ref, out_ref):
    total = jnp.sum(got_ref[...], axis=0)
    for c in range(out_ref.shape[0]):
        out_ref[c] = total


def advance(pick, quad_ref, solved_ref, heads_ref, lines_ref, diag_ref, heads_out, y_out):
    group = solved_ref.shape[0]
    left = lines_ref.shape[0]
    rows = diag_ref.shape[2]
    if pick:
        quad = quad_ref[0]
        x = jnp.concatenate([solved_ref[s, quad] for s in range(group)], axis=1)
    else:
        x = jnp.concatenate([solved_ref[s] for s in range(group)], axis=1)
    base = heads_ref.shape[0] - left
    head = None
    for b in range(left):
        new = heads_ref[base + b] - dot(x, lines_ref[b], NN)
        heads_out[b] = new
        if b == 0:
            head = new
    y = dot(head, diag_ref[0], NT)
    for s in range(group):
        y_out[s] = y[:, s * rows : (s + 1) * rows]


def gathered_first(x_ref, pair):
    parts = [x_ref[:, 0, s] if len(x_ref.shape) == 5 else x_ref[s] for s in range(pair)]
    parts = [p.reshape(-1, p.shape[-1]) for p in parts]
    return jnp.concatenate(parts, axis=1)


def trail_sum(x_ref, f_ref, out_ref):
    @pl.when(pl.program_id(0) == 0)
    def _():
        out_ref[...] = jnp.zeros_like(out_ref)

    out_ref[...] += dot(gathered_first(x_ref, 2), f_ref[0, 0], NN)


def trail_more(x_ref, f_ref, init_ref, out_ref):
    @pl.when(pl.program_id(0) == 0)
    def _():
        out_ref[...] = init_ref[...]

    out_ref[...] += dot(gathered_first(x_ref, 2), f_ref[0, 0], NN)


def trail_end(x_ref, f_ref, init_ref, r_ref, out_ref, acc_ref):
    @pl.when(pl.program_id(0) == 0)
    def _():
        acc_ref[...] = init_ref[...]

    acc_ref[...] += dot(gathered_first(x_ref, 2), f_ref[0, 0], NN)

    @pl.when(pl.program_id(0) == pl.num_programs(0) - 1)
    def _():
        n = out_ref.shape[0]
        out_ref[...] = r_ref[r_ref.shape[0] - n :] - acc_ref[...].T


def trail_call(kernel, x, f, k, steps, out_shape, extra=(), scratch=()):
    per_pair = f.shape[2] // 256
    per_panel = f.shape[1] * per_pair
    if x.ndim == 5:
        x_spec = pl.BlockSpec(
            (x.shape[0], 1, 2, *x.shape[3:]), lambda i: (0, i // per_panel, i % per_panel, 0, 0)
        )
    else:
        x_spec = pl.BlockSpec((2, *x.shape[1:]), lambda i: (i % per_panel, 0, 0, 0))
    f_spec = pl.BlockSpec(
        (1, 1, 256, f.shape[3]),
        lambda i: (k + i // per_panel, (i % per_panel) // per_pair, i % per_pair, 0),
    )
    return pl.pallas_call(
        kernel,
        out_shape=jax.ShapeDtypeStruct(out_shape, F32),
        grid=(steps * per_panel,),
        in_specs=[x_spec, f_spec] + [whole(e.shape) for e in extra],
        out_specs=whole(out_shape),
        scratch_shapes=scratch,
    )(x, f, *extra)


def spread(array, axes):
    return lax.all_to_all(
        jnp.broadcast_to(array[None], (lax.axis_size(axes), *array.shape)), axes, 0, 0, tiled=True
    )


def body(factor, inverses, right_side):
    lower = jnp.transpose(factor[0], (1, 2, 0))
    inv = jnp.transpose(inverses[0], (0, 2, 1))
    current = right_side[0]
    panels, cols, _ = lower.shape
    width = inv.shape[1]
    count = current.shape[1]
    tail = panels * width
    quads = lax.axis_size("yq")
    nx, npair = lax.axis_size("x"), lax.axis_size("yp")
    blocks = lax.axis_size(RHS)
    group = nx * npair
    per = count // quads
    rows = quads * width
    half = cols // npair
    quad = lax.axis_index("yq")

    (sent,) = call(
        pack,
        [(quads, per + 2 * cols + half, tail)],
        [whole((panels, cols, tail)), whole(inv.shape), whole((tail, count))],
    )(lower, inv, current)
    got = lax.all_to_all(sent, "yq", 0, 0, tiled=True)
    heads, pay, first = call(
        lambda *refs: sort(width, per, *refs),
        [(panels, per, rows), (9, npair, half, rows), (blocks, npair, half, rows)],
        [whole(sent.shape)],
    )(got)
    first = lax.all_to_all(first, RHS, 0, 0, tiled=True)
    rest = lax.all_gather(pay, RHS, axis=2, tiled=True)
    trail = lower[:, :, tail:].reshape(panels, npair, half, -1)
    trail = lax.all_gather(trail, RHS, axis=2, tiled=True)
    rest = rest.reshape(9, group * rows, rows)

    (y,) = call(
        begin,
        [(group, per, rows)],
        [pl.BlockSpec((1, per, rows), lambda i: (0, 0, 0)), whole(first.shape)],
    )(heads, first)
    block = (group, per, rows)
    early, own, late = [], [], []
    for k in range(panels):
        got = lax.all_to_all(y, GROUP, 0, 0, tiled=True)
        direct = k < 2
        copies = group if direct else quads
        (mine,) = call(add_up, [(copies, per, rows)], [whole(block)])(got)
        if direct:
            solved = lax.all_to_all(mine, GROUP, 0, 0, tiled=True)
            early.append(solved)
        else:
            mine = lax.all_to_all(mine, "yq", 0, 0, tiled=True)
            own.append(mine)
            solved = spread(mine, GROUP)
            late.append(solved)
        if k == panels - 1:
            break
        left = panels - 1 - k
        at = {3: 1, 2: 3, 1: 8}[left]
        heads, y = call(
            lambda *refs, p=not direct: advance(p, *refs),
            [(left, per, rows), block],
            [
                pl.BlockSpec(memory_space=pltpu.SMEM),
                whole(solved.shape),
                whole(heads.shape),
                pl.BlockSpec((left, group * rows, rows), lambda i, at=at: (at, 0, 0)),
                pl.BlockSpec((1, group * rows, rows), lambda i, k=k: (k, 0, 0)),
            ],
        )(quad.reshape(1).astype(jnp.int32), solved, heads, rest, rest)

    early = jnp.stack(early)
    early = lax.all_gather(early, "yq", axis=0)

    place = lax.axis_index("yp") * nx + lax.axis_index("x")
    acc_shape = (count, trail.shape[3])
    acc = trail_call(trail_sum, early, trail, 0, 2, acc_shape)
    acc = trail_call(trail_more, late[0], trail, 2, 1, acc_shape, (acc,))
    out = trail_call(
        trail_end, late[1], trail, 3, 1, (trail.shape[3], count), (acc, current),
        [pltpu.VMEM(acc_shape, F32)],
    )
    pieces = lax.dynamic_index_in_dim(early, place, 2, keepdims=False)
    pieces = jnp.concatenate([jnp.swapaxes(pieces, 0, 1), jnp.stack(own)], axis=0)
    pieces = lax.dynamic_slice_in_dim(pieces, quad * width, width, 3)
    mine = jnp.transpose(pieces, (0, 3, 1, 2)).reshape(tail, count)
    return (mine[None], out[None])


def solution(mesh):
    nx, ny, nz, nc = SIZES(mesh)
    fine = Mesh(
        mesh.devices.reshape(nx, QUADS, ny // QUADS, nz, nc), ("x", "yq", "yp", "z", "core")
    )
    row = ("x", "yq", "yp")
    in_specs = (P(row, None, None, RHS), P(row, None, RHS, None), P(row, None, RHS))
    out_specs = (P(row, None, RHS), P(row, None, RHS))
    return jax.shard_map(body, mesh=fine, in_specs=in_specs, out_specs=out_specs, check_vma=False)


def SIZES(mesh):
    nrow, nrhs = mesh.shape["row"], mesh.shape["rhs"]
    return nrow // 8, 8, nrhs // 2, 2
```

```python
import jax
import jax.numpy as jnp
from jax import lax
from jax.experimental import pallas as pl
from jax.experimental.pallas import tpu as pltpu
from jax.sharding import Mesh, PartitionSpec as P

QUADS = 4
DIRECT = ()
RHS = ("z", "core")
GROUP = ("yp", "x")
F32 = jnp.float32


def halves(value):
    high = value.astype(jnp.bfloat16)
    return high, (value - high.astype(F32)).astype(jnp.bfloat16)


def dot(a, b, dims):
    def one(u, v):
        return lax.dot_general(u, v, (dims, ((), ())), preferred_element_type=F32)

    ah, al = halves(a)
    bh, bl = halves(b)
    return one(ah, bh) + (one(ah, bl) + one(al, bh))


NN = ((1,), (0,))
NT = ((1,), (1,))


VMEM = pl.BlockSpec(memory_space=pltpu.VMEM)
SMEM = pl.BlockSpec(memory_space=pltpu.SMEM)
HBM = pl.BlockSpec(memory_space=pltpu.HBM)


def call(kernel, shapes, in_specs, scratch=(), limit=20 << 20):
    return pl.pallas_call(
        kernel,
        out_shape=[jax.ShapeDtypeStruct(s, F32) for s in shapes],
        in_specs=in_specs,
        out_specs=[VMEM] * len(shapes),
        scratch_shapes=scratch,
        compiler_params=pltpu.CompilerParams(vmem_limit_bytes=limit),
    )


def whole(shape):
    return pl.BlockSpec(shape, lambda i: (0,) * len(shape))


def pack(f_ref, inv_ref, r_ref, out_ref):
    quads, _, _ = out_ref.shape
    cols = f_ref.shape[1]
    per = r_ref.shape[1] // quads
    w = inv_ref.shape[1]
    turned = r_ref[...].T
    wide = jnp.concatenate([f_ref[0][:, w:], f_ref[2][:, 3 * w :]], axis=1)
    mid = f_ref[1][:, 2 * w :]
    mid = jnp.concatenate([mid[: cols // 2], mid[cols // 2 :]], axis=1)
    diag = jnp.concatenate([inv_ref[k].T for k in range(4)], axis=1)
    for q in range(quads):
        out_ref[q, :per] = turned[q * per : (q + 1) * per]
        out_ref[q, per : per + cols] = wide
        out_ref[q, per + cols : per + cols + cols // 2] = mid
        out_ref[q, per + cols + cols // 2 :] = diag


def sort(w, per, got_ref, heads_ref, pay_ref, first_ref):
    quads = got_ref.shape[0]
    half = pay_ref.shape[2]
    cols = 2 * half
    a, b, d = per, per + cols, per + cols + half

    def lanes(start, n, at):
        return jnp.concatenate(
            [got_ref[q, start : start + n][:, at : at + w] for q in range(quads)], axis=1
        )

    for k in range(4):
        heads_ref[k] = lanes(0, per, k * w)
    for h in range(2):
        for k in range(1, 4):
            pay_ref[k - 1, h] = lanes(d + h * half, half, k * w)
        for j in range(3):
            pay_ref[3 + j, h] = lanes(a + h * half, half, j * w)
        for j in range(2):
            pay_ref[6 + j, h] = lanes(b, half, h * 2 * w + j * w)
        pay_ref[8, h] = lanes(a + h * half, half, 3 * w)
        piece = lanes(d + h * half, half, 0)
        for c in range(first_ref.shape[0]):
            first_ref[c, h] = piece


def begin(head_ref, first_ref, out_ref):
    blocks, pair, half, rows = first_ref.shape
    head = head_ref[0]
    for p in range(pair):
        block = first_ref[:, p].reshape(blocks * half, rows)
        y = dot(head, block, NT)
        n = blocks * half // rows
        for x in range(n):
            out_ref[p * n + x] = y[:, x * rows : (x + 1) * rows]


def add_up(got_ref, out_ref):
    total = jnp.sum(got_ref[...], axis=0)
    for c in range(out_ref.shape[0]):
        out_ref[c] = total


def advance(at, diag_at, quad_ref, solved_ref, heads_ref, rest_ref, heads_out, y_out,
            lines_ref, diag_ref, sems):
    group, rows = y_out.shape[0], y_out.shape[2]
    left = lines_ref.shape[0]
    first = pltpu.make_async_copy(rest_ref.at[pl.ds(at, left)], lines_ref, sems.at[0])
    second = pltpu.make_async_copy(rest_ref.at[diag_at], diag_ref, sems.at[1])
    first.start()
    second.start()
    if len(solved_ref.shape) == 4:
        quad = quad_ref[0]
        x = jnp.concatenate([solved_ref[s, quad] for s in range(group)], axis=1)
    else:
        x = jnp.concatenate([solved_ref[s] for s in range(group)], axis=1)
    base = heads_ref.shape[0] - left
    first.wait()
    for b in range(left):
        heads_out[b] = heads_ref[base + b] - dot(x, lines_ref[b], NN)
    second.wait()
    y = dot(heads_out[0], diag_ref[...], NT)
    for s in range(group):
        y_out[s] = y[:, s * rows : (s + 1) * rows]


def stacked(x_refs):
    if len(x_refs) == 1:
        parts = [x_refs[0][s].reshape(-1, x_refs[0].shape[-1]) for s in range(2)]
    else:
        parts = [jnp.concatenate([x[0, s] for x in x_refs], axis=0) for s in range(2)]
    return jnp.concatenate(parts, axis=1)


def trail_sum(n, *refs):
    x_refs, f_ref, out_ref = refs[:n], refs[n], refs[-1]

    @pl.when(pl.program_id(0) == 0)
    def _():
        out_ref[...] = jnp.zeros_like(out_ref) if len(refs) == n + 2 else refs[n + 1][...]

    out_ref[...] += dot(stacked(x_refs), f_ref[0, 0], NN)


def trail_end(x_ref, f_ref, acc_ref, turn_ref, quad_ref, r_ref, out_ref, sum_ref):
    quads, per, _ = turn_ref.shape

    @pl.when(pl.program_id(0) == 0)
    def _():
        for q in range(quads):
            at = lax.rem(q + quads - quad_ref[0], quads)
            sum_ref[q * per : (q + 1) * per] = (
                acc_ref[q * per : (q + 1) * per] + turn_ref[at]
            )

    sum_ref[...] += dot(stacked([x_ref]), f_ref[0, 0], NN)

    @pl.when(pl.program_id(0) == pl.num_programs(0) - 1)
    def _():
        n = out_ref.shape[0]
        out_ref[...] = r_ref[r_ref.shape[0] - n :] - sum_ref[...].T


def trail_call(kernel, x, f, k, out_shape, extra=(), specs=(), steps=1, scratch=()):
    per_pair = f.shape[2] // 256
    per_panel = f.shape[1] * per_pair
    if len(x) == 1:
        x_specs = [pl.BlockSpec((2, *x[0].shape[1:]), lambda i: (i % per_panel, 0, 0, 0))]
    else:
        x_specs = [
            pl.BlockSpec((1, 2, *p.shape[2:]), lambda i: (i // per_panel, i % per_panel, 0, 0))
            for p in x
        ]
    f_spec = pl.BlockSpec(
        (1, 1, 256, f.shape[3]),
        lambda i: (k + i // per_panel, (i % per_panel) // per_pair, i % per_pair, 0),
    )
    return pl.pallas_call(
        kernel,
        out_shape=jax.ShapeDtypeStruct(out_shape, F32),
        grid=(steps * per_panel,),
        in_specs=[*x_specs, f_spec, *specs],
        out_specs=whole(out_shape),
        scratch_shapes=scratch,
        compiler_params=pltpu.CompilerParams(vmem_limit_bytes=56 << 20),
    )(*x, f, *extra)


def spread(array, axes):
    return lax.all_to_all(
        jnp.broadcast_to(array[None], (lax.axis_size(axes), *array.shape)), axes, 0, 0, tiled=True
    )


def body(factor, inverses, right_side):
    lower = jnp.transpose(factor[0], (1, 2, 0))
    inv = jnp.transpose(inverses[0], (0, 2, 1))
    current = right_side[0]
    panels, cols, _ = lower.shape
    width = inv.shape[1]
    count = current.shape[1]
    tail = panels * width
    quads = lax.axis_size("yq")
    nx, npair = lax.axis_size("x"), lax.axis_size("yp")
    blocks = lax.axis_size(RHS)
    group = nx * npair
    per = count // quads
    rows = quads * width
    half = cols // npair
    quad = lax.axis_index("yq")

    index = quad.reshape(1).astype(jnp.int32)
    corner = lower[:, :, :tail]
    (sent,) = call(
        pack, [(quads, per + 2 * cols + half, tail)], [VMEM, VMEM, VMEM]
    )(corner, inv, current[:tail])
    got = lax.all_to_all(sent, "yq", 0, 0, tiled=True)
    heads, pay, first = call(
        lambda *refs: sort(width, per, *refs),
        [(panels, per, rows), (9, npair, half, rows), (blocks, npair, half, rows)],
        [VMEM],
    )(got)
    first = lax.all_to_all(first, RHS, 0, 0, tiled=True)
    pay, first = lax.optimization_barrier((pay, first))
    rest = lax.all_gather(pay, RHS, axis=2, tiled=True)
    trail = lower[:, :, tail:].reshape(panels, npair, half, -1)
    trail = lax.all_gather(trail, RHS, axis=2, tiled=True)
    rest = rest.reshape(9, group * rows, rows)

    (y,) = call(begin, [(group, per, rows)], [VMEM, VMEM])(heads, first)
    block = (group, per, rows)
    acc_shape = (count, trail.shape[3])
    direct, own, late = [], {}, {}

    def add_trail(acc, k):
        more = () if acc is None else (acc,)
        return trail_call(
            lambda *refs: trail_sum(1, *refs), [late[k]], trail, k, acc_shape,
            more, (whole(acc_shape),) * len(more),
        )

    acc = None
    for k in range(panels):
        got = lax.all_to_all(y, GROUP, 0, 0, tiled=True)
        copies = group if k in DIRECT else quads
        (mine,) = call(add_up, [(copies, per, rows)], [VMEM])(got)
        if k in DIRECT:
            solved = lax.all_to_all(mine, GROUP, 0, 0, tiled=True)
            direct.append(solved)
        else:
            mine = lax.all_to_all(mine, "yq", 0, 0, tiled=True)
            if k == 3 and not DIRECT:
                acc = add_trail(acc, 1)
                mine, acc = lax.optimization_barrier((mine, acc))
            own[k] = mine
            solved = spread(mine, GROUP)
            if k == 2 and not DIRECT:
                acc = add_trail(acc, 0)
                solved, acc = lax.optimization_barrier((solved, acc))
            late[k] = solved
        if k == panels - 1:
            break
        left = panels - 1 - k
        at = {3: 3, 2: 6, 1: 8}[left]
        heads, y = call(
            lambda *refs, at=at, k=k: advance(at, k, *refs),
            [(left, per, rows), block],
            [SMEM, VMEM, VMEM, HBM],
            [
                pltpu.VMEM((left, group * rows, rows), F32),
                pltpu.VMEM((group * rows, rows), F32),
                pltpu.SemaphoreType.DMA((2,)),
            ],
            limit=63_000_000,
        )(index, solved, heads, rest)

    place = lax.axis_index("yp") * nx + lax.axis_index("x")
    turn = jnp.zeros((quads, per, trail.shape[3]), F32)
    if DIRECT:
        direct = jnp.stack(direct)
        parts = [direct] + [
            lax.ppermute(direct, "yq", [(i, (i - t) % quads) for i in range(quads)])
            for t in range(1, quads)
        ]
        turn = trail_call(
            lambda *refs: trail_sum(quads, *refs), parts, trail, DIRECT[0], acc_shape,
            steps=len(DIRECT),
        ).reshape(turn.shape)
        pieces = jnp.stack(
            [lax.dynamic_index_in_dim(p, place, 1, keepdims=False) for p in parts]
        )
        pieces = jnp.concatenate([pieces, pieces], axis=0)
        pieces = lax.dynamic_slice_in_dim(pieces, (quads - quad) % quads, quads, 0)
        for n, k in enumerate(DIRECT):
            own[k] = pieces[:, n]
    for k in (0,) if DIRECT else (2,):
        acc = add_trail(acc, k)
    out = trail_call(
        trail_end, [late[panels - 1]], trail, panels - 1, (trail.shape[3], count),
        (acc, turn, index, current),
        (whole(acc_shape), whole(turn.shape), SMEM, whole(current.shape)),
        scratch=[pltpu.VMEM(acc_shape, F32)],
    )
    pieces = jnp.stack([own[k] for k in range(panels)])
    pieces = lax.dynamic_slice_in_dim(pieces, quad * width, width, 3)
    mine = jnp.transpose(pieces, (0, 3, 1, 2)).reshape(tail, count)
    return (mine[None], out[None])


def solution(mesh):
    nx, ny, nz, nc = SIZES(mesh)
    fine = Mesh(
        mesh.devices.reshape(nx, QUADS, ny // QUADS, nz, nc), ("x", "yq", "yp", "z", "core")
    )
    row = ("x", "yq", "yp")
    in_specs = (P(row, None, None, RHS), P(row, None, RHS, None), P(row, None, RHS))
    out_specs = (P(row, None, RHS), P(row, None, RHS))
    return jax.shard_map(body, mesh=fine, in_specs=in_specs, out_specs=out_specs, check_vma=False)


def SIZES(mesh):
    nrow, nrhs = mesh.shape["row"], mesh.shape["rhs"]
    return nrow // 8, 8, nrhs // 2, 2
```

```python
import jax
import jax.numpy as jnp
from jax import lax
from jax.experimental import pallas as pl
from jax.experimental.pallas import tpu as pltpu
from jax.sharding import Mesh, PartitionSpec as P

QUADS = 4
RHS = ("z", "core")
GROUP = ("yp", "x")
F32 = jnp.float32


def halves(value):
    high = value.astype(jnp.bfloat16)
    return high, (value - high.astype(F32)).astype(jnp.bfloat16)


def dot(a, b, dims):
    def one(u, v):
        return lax.dot_general(u, v, (dims, ((), ())), preferred_element_type=F32)

    ah, al = halves(a)
    bh, bl = halves(b)
    return one(ah, bh) + (one(ah, bl) + one(al, bh))


NN = ((1,), (0,))
NT = ((1,), (1,))


VMEM = pl.BlockSpec(memory_space=pltpu.VMEM)
SMEM = pl.BlockSpec(memory_space=pltpu.SMEM)
HBM = pl.BlockSpec(memory_space=pltpu.HBM)


def call(kernel, shapes, in_specs, scratch=()):
    return pl.pallas_call(
        kernel,
        out_shape=[jax.ShapeDtypeStruct(s, F32) for s in shapes],
        in_specs=in_specs,
        out_specs=[VMEM] * len(shapes),
        scratch_shapes=scratch,
        compiler_params=pltpu.CompilerParams(vmem_limit_bytes=20 << 20),
    )


def in_hbm(array):
    return pltpu.with_memory_space_constraint(array, pltpu.HBM)


def whole(shape):
    return pl.BlockSpec(shape, lambda i: (0,) * len(shape))


def pack(f_hbm, inv_hbm, r_hbm, out_ref, f_ref, inv_ref, r_ref, sems):
    quads, _, lanes = out_ref.shape
    copies = [
        pltpu.make_async_copy(f_hbm.at[:, :, pl.ds(0, lanes)], f_ref, sems.at[0]),
        pltpu.make_async_copy(inv_hbm, inv_ref, sems.at[1]),
        pltpu.make_async_copy(r_hbm.at[pl.ds(0, lanes)], r_ref, sems.at[2]),
    ]
    for c in copies:
        c.start()
    for c in copies:
        c.wait()
    cols = f_ref.shape[1]
    per = r_ref.shape[1] // quads
    w = inv_ref.shape[1]
    turned = r_ref[...].T
    wide = jnp.concatenate([f_ref[0][:, w:], f_ref[2][:, 3 * w :]], axis=1)
    mid = f_ref[1][:, 2 * w :]
    mid = jnp.concatenate([mid[: cols // 2], mid[cols // 2 :]], axis=1)
    diag = jnp.concatenate([inv_ref[k].T for k in range(4)], axis=1)
    for q in range(quads):
        out_ref[q, :per] = turned[q * per : (q + 1) * per]
        out_ref[q, per : per + cols] = wide
        out_ref[q, per + cols : per + cols + cols // 2] = mid
        out_ref[q, per + cols + cols // 2 :] = diag


def sort(w, per, got_ref, heads_ref, pay_ref, first_ref):
    quads = got_ref.shape[0]
    half = pay_ref.shape[2]
    cols = 2 * half
    a, b, d = per, per + cols, per + cols + half

    def lanes(start, n, at):
        return jnp.concatenate(
            [got_ref[q, start : start + n][:, at : at + w] for q in range(quads)], axis=1
        )

    for k in range(4):
        heads_ref[k] = lanes(0, per, k * w)
    for h in range(2):
        for k in range(1, 4):
            pay_ref[k - 1, h] = lanes(d + h * half, half, k * w)
        for j in range(3):
            pay_ref[3 + j, h] = lanes(a + h * half, half, j * w)
        for j in range(2):
            pay_ref[6 + j, h] = lanes(b, half, h * 2 * w + j * w)
        pay_ref[8, h] = lanes(a + h * half, half, 3 * w)
        piece = lanes(d + h * half, half, 0)
        for c in range(first_ref.shape[0]):
            first_ref[c, h] = piece


def begin(head_ref, first_ref, out_ref):
    blocks, pair, half, rows = first_ref.shape
    head = head_ref[0]
    for p in range(pair):
        block = first_ref[:, p].reshape(blocks * half, rows)
        y = dot(head, block, NT)
        n = blocks * half // rows
        for x in range(n):
            out_ref[p * n + x] = y[:, x * rows : (x + 1) * rows]


def add_up(got_ref, out_ref):
    total = jnp.sum(got_ref[...], axis=0)
    for c in range(out_ref.shape[0]):
        out_ref[c] = total


def advance(base, at, diag_at, quad_ref, solved_ref, head_ref, rest_hbm, y_out, line_ref, diag_ref, sems):
    group, rows = y_out.shape[0], y_out.shape[2]
    first = pltpu.make_async_copy(rest_hbm.at[at], line_ref, sems.at[0])
    second = pltpu.make_async_copy(rest_hbm.at[diag_at], diag_ref, sems.at[1])
    first.start()
    second.start()
    x = chosen(quad_ref, solved_ref)
    first.wait()
    head = head_ref[base] - dot(x, line_ref[...], NN)
    second.wait()
    y = dot(head, diag_ref[...], NT)
    for s in range(group):
        y_out[s] = y[:, s * rows : (s + 1) * rows]


def chosen(quad_ref, solved_ref):
    quad = quad_ref[0]
    return jnp.concatenate([solved_ref[s, quad] for s in range(solved_ref.shape[0])], axis=1)


def follow(base, at, quad_ref, solved_ref, heads_ref, rest_hbm, heads_out, lines_ref, sem):
    left = heads_out.shape[0]
    copy = pltpu.make_async_copy(rest_hbm.at[pl.ds(at, left)], lines_ref, sem)
    copy.start()
    x = chosen(quad_ref, solved_ref)
    copy.wait()
    for b in range(left):
        heads_out[b] = heads_ref[base + b + 1] - dot(x, lines_ref[b], NN)


def stacked(x_refs):
    if len(x_refs) == 1:
        parts = [x_refs[0][s].reshape(-1, x_refs[0].shape[-1]) for s in range(2)]
    else:
        parts = [jnp.concatenate([x[0, s] for x in x_refs], axis=0) for s in range(2)]
    return jnp.concatenate(parts, axis=1)


def trail_sum(n, *refs):
    x_refs, f_ref, init_ref, out_ref = refs[:n], refs[n], refs[n + 1], refs[-1]

    @pl.when(pl.program_id(0) == 0)
    def _():
        if init_ref.shape == out_ref.shape:
            out_ref[...] = init_ref[...]
        else:
            out_ref[...] = init_ref[init_ref.shape[0] - out_ref.shape[1] :].T

    out_ref[...] -= dot(stacked(x_refs), f_ref[0, 0], NN)


def finish(panel, x_ref, f_hbm, base_ref, quad_ref, *refs):
    own_refs, (out_ref, mine_ref, turned_ref, f_ref, sems) = refs[:-5], refs[-5:]
    n = f_ref.shape[0]
    copies = [
        pltpu.make_async_copy(f_hbm.at[panel, b], f_ref.at[b], sems.at[b]) for b in range(n)
    ]
    for c in copies:
        c.start()
    width = mine_ref.shape[0] // len(own_refs)
    at = pl.multiple_of(quad_ref[0] * width, width)
    for k, own_ref in enumerate(own_refs):
        turned_ref[...] = own_ref[...].reshape(-1, own_ref.shape[2]).T
        mine_ref[k * width : (k + 1) * width] = turned_ref[pl.ds(at, width)]
    total = base_ref[...]
    for b, c in enumerate(copies):
        c.wait()
        total -= dot(stacked([x_ref.at[pl.ds(2 * b, 2)]]), f_ref[b], NN)
    out_ref[...] = total.T


def trail_call(kernel, x, f, k, out_shape, extra=(), specs=(), steps=1, scratch=()):
    per_pair = f.shape[2] // 256
    per_panel = f.shape[1] * per_pair
    if len(x) == 1:
        x_specs = [pl.BlockSpec((2, *x[0].shape[1:]), lambda i: (i % per_panel, 0, 0, 0))]
    else:
        x_specs = [
            pl.BlockSpec((1, 2, *p.shape[2:]), lambda i: (i // per_panel, i % per_panel, 0, 0))
            for p in x
        ]
    f_spec = pl.BlockSpec(
        (1, 1, 256, f.shape[3]),
        lambda i: (k + i // per_panel, (i % per_panel) // per_pair, i % per_pair, 0),
    )
    return pl.pallas_call(
        kernel,
        out_shape=jax.ShapeDtypeStruct(out_shape, F32),
        grid=(steps * per_panel,),
        in_specs=[*x_specs, f_spec, *specs],
        out_specs=whole(out_shape),
        scratch_shapes=scratch,
        compiler_params=pltpu.CompilerParams(vmem_limit_bytes=16 << 20),
    )(*x, in_hbm(f), *extra)


def spread(array, axes):
    return lax.all_to_all(
        jnp.broadcast_to(array[None], (lax.axis_size(axes), *array.shape)), axes, 0, 0, tiled=True
    )


def body(factor, inverses, right_side):
    lower = jnp.transpose(factor[0], (1, 2, 0))
    inv = jnp.transpose(inverses[0], (0, 2, 1))
    current = right_side[0]
    panels, cols, _ = lower.shape
    width = inv.shape[1]
    count = current.shape[1]
    tail = panels * width
    quads = lax.axis_size("yq")
    nx, npair = lax.axis_size("x"), lax.axis_size("yp")
    blocks = lax.axis_size(RHS)
    group = nx * npair
    per = count // quads
    rows = quads * width
    half = cols // npair
    quad = lax.axis_index("yq")

    index = quad.reshape(1).astype(jnp.int32)
    (sent,) = call(
        pack,
        [(quads, per + 2 * cols + half, tail)],
        [HBM, HBM, HBM],
        [
            pltpu.VMEM((panels, cols, tail), F32),
            pltpu.VMEM(inv.shape, F32),
            pltpu.VMEM((tail, count), F32),
            pltpu.SemaphoreType.DMA((3,)),
        ],
    )(in_hbm(lower), in_hbm(inv), in_hbm(current))
    got = lax.all_to_all(sent, "yq", 0, 0, tiled=True)
    heads, pay, first = call(
        lambda *refs: sort(width, per, *refs),
        [(panels, per, rows), (9, npair, half, rows), (blocks, npair, half, rows)],
        [VMEM],
    )(got)
    first = lax.all_to_all(first, RHS, 0, 0, tiled=True)
    pay, first = lax.optimization_barrier((pay, first))
    rest = lax.all_gather(pay, RHS, axis=2, tiled=True)
    rest = rest.reshape(9, group * rows, rows)

    (y,) = call(begin, [(group, per, rows)], [VMEM, VMEM])(heads, first)
    length = lower.shape[2] - tail
    own, late = {}, {}
    trail = base = None
    for k in range(panels):
        got = lax.all_to_all(y, GROUP, 0, 0, tiled=True)
        if k == 3:
            base = add_trail(late[1], trail, 1, base)
            got, base = lax.optimization_barrier((got, base))
        (mine,) = call(add_up, [(quads, per, rows)], [VMEM])(got)
        if k == 0:
            lower, mine = lax.optimization_barrier((lower, mine))
            trail = lower[:, :, tail:].reshape(panels, npair, half, -1)
            trail = lax.all_gather(trail, RHS, axis=2, tiled=True)
        mine = lax.all_to_all(mine, "yq", 0, 0, tiled=True)
        if k == 3:
            base = add_trail(late[2], trail, 2, base)
            mine, base = lax.optimization_barrier((mine, base))
        own[k] = mine
        solved = spread(mine, GROUP)
        if k == 2:
            base = add_trail(late[0], trail, 0, current)
            solved, base = lax.optimization_barrier((solved, base))
        late[k] = solved
        if k == panels - 1:
            break
        left = panels - 1 - k
        at = {3: 3, 2: 6, 1: 8}[left]
        one = pltpu.VMEM((group * rows, rows), F32)
        (y,) = call(
            lambda *refs, at=at, k=k: advance(int(k == 0), at, k, *refs),
            [(group, per, rows)],
            [SMEM, VMEM, VMEM, HBM],
            [one, one, pltpu.SemaphoreType.DMA((2,))],
        )(index, solved, heads, in_hbm(rest))
        if left > 1:
            (heads,) = call(
                lambda *refs, at=at, k=k: follow(int(k == 0), at + 1, *refs),
                [(left - 1, per, rows)],
                [SMEM, VMEM, VMEM, HBM],
                [
                    pltpu.VMEM((left - 1, group * rows, rows), F32),
                    pltpu.SemaphoreType.DMA,
                ],
            )(index, solved, heads, in_hbm(rest))

    flat = trail.reshape(panels, -1, 2 * rows, length)
    out, mine = call(
        lambda *refs: finish(panels - 1, *refs),
        [(length, count), (tail, count)],
        [VMEM, HBM, VMEM, SMEM] + [VMEM] * panels,
        [
            pltpu.VMEM((rows, count), F32),
            pltpu.VMEM(flat.shape[1:], F32),
            pltpu.SemaphoreType.DMA((flat.shape[1],)),
        ],
    )(late[3], in_hbm(flat), base, index, *[own[k] for k in range(panels)])
    return (mine[None], out[None])


def add_trail(x, trail, k, init):
    shape = (x.shape[1] * x.shape[2], trail.shape[3])
    return trail_call(
        lambda *refs: trail_sum(1, *refs), [x], trail, k, shape, (init,), (whole(init.shape),)
    )


def solution(mesh):
    nx, ny, nz, nc = SIZES(mesh)
    fine = Mesh(
        mesh.devices.reshape(nx, QUADS, ny // QUADS, nz, nc), ("x", "yq", "yp", "z", "core")
    )
    row = ("x", "yq", "yp")
    in_specs = (P(row, None, None, RHS), P(row, None, RHS, None), P(row, None, RHS))
    out_specs = (P(row, None, RHS), P(row, None, RHS))
    return jax.shard_map(body, mesh=fine, in_specs=in_specs, out_specs=out_specs, check_vma=False)


def SIZES(mesh):
    nrow, nrhs = mesh.shape["row"], mesh.shape["rhs"]
    return nrow // 8, 8, nrhs // 2, 2
```

```python
import jax
import jax.numpy as jnp
from jax import lax
from jax.experimental import pallas as pl
from jax.experimental.pallas import tpu as pltpu
from jax.sharding import Mesh, PartitionSpec as P

QUADS = 4
BATCHES = ((0, 1), (2,))
RHS = ("z", "core")
GROUP = ("yp", "x")
F32 = jnp.float32


def halves(value):
    high = value.astype(jnp.bfloat16)
    return high, (value - high.astype(F32)).astype(jnp.bfloat16)


def dot(a, b, dims):
    def one(u, v):
        return lax.dot_general(u, v, (dims, ((), ())), preferred_element_type=F32)

    ah, al = halves(a)
    bh, bl = halves(b)
    return one(ah, bh) + (one(ah, bl) + one(al, bh))


NN = ((1,), (0,))
NT = ((1,), (1,))


VMEM = pl.BlockSpec(memory_space=pltpu.VMEM)
SMEM = pl.BlockSpec(memory_space=pltpu.SMEM)
HBM = pl.BlockSpec(memory_space=pltpu.HBM)


def call(kernel, shapes, in_specs, scratch=()):
    return pl.pallas_call(
        kernel,
        out_shape=[jax.ShapeDtypeStruct(s, F32) for s in shapes],
        in_specs=in_specs,
        out_specs=[VMEM] * len(shapes),
        scratch_shapes=scratch,
        compiler_params=pltpu.CompilerParams(vmem_limit_bytes=20 << 20),
    )


def in_hbm(array):
    return pltpu.with_memory_space_constraint(array, pltpu.HBM)


def whole(shape):
    return pl.BlockSpec(shape, lambda i: (0,) * len(shape))


def pack(f_hbm, inv_hbm, r_hbm, out_ref, f_ref, inv_ref, r_ref, sems):
    quads, _, lanes = out_ref.shape
    copies = [
        pltpu.make_async_copy(f_hbm.at[:, :, pl.ds(0, lanes)], f_ref, sems.at[0]),
        pltpu.make_async_copy(inv_hbm, inv_ref, sems.at[1]),
        pltpu.make_async_copy(r_hbm.at[pl.ds(0, lanes)], r_ref, sems.at[2]),
    ]
    for c in copies:
        c.start()
    for c in copies:
        c.wait()
    cols = f_ref.shape[1]
    per = r_ref.shape[1] // quads
    w = inv_ref.shape[1]
    turned = r_ref[...].T
    wide = jnp.concatenate([f_ref[0][:, w:], f_ref[2][:, 3 * w :]], axis=1)
    mid = f_ref[1][:, 2 * w :]
    mid = jnp.concatenate([mid[: cols // 2], mid[cols // 2 :]], axis=1)
    diag = jnp.concatenate([inv_ref[k].T for k in range(4)], axis=1)
    for q in range(quads):
        out_ref[q, :per] = turned[q * per : (q + 1) * per]
        out_ref[q, per : per + cols] = wide
        out_ref[q, per + cols : per + cols + cols // 2] = mid
        out_ref[q, per + cols + cols // 2 :] = diag


def sort(w, per, got_ref, heads_ref, pay_ref, first_ref):
    quads = got_ref.shape[0]
    half = pay_ref.shape[2]
    cols = 2 * half
    a, b, d = per, per + cols, per + cols + half

    def lanes(start, n, at):
        return jnp.concatenate(
            [got_ref[q, start : start + n][:, at : at + w] for q in range(quads)], axis=1
        )

    for k in range(4):
        heads_ref[k] = lanes(0, per, k * w)
    for h in range(2):
        for k in range(1, 4):
            pay_ref[k - 1, h] = lanes(d + h * half, half, k * w)
        for j in range(3):
            pay_ref[3 + j, h] = lanes(a + h * half, half, j * w)
        for j in range(2):
            pay_ref[6 + j, h] = lanes(b, half, h * 2 * w + j * w)
        pay_ref[8, h] = lanes(a + h * half, half, 3 * w)
        piece = lanes(d + h * half, half, 0)
        for c in range(first_ref.shape[0]):
            first_ref[c, h] = piece


def begin(head_ref, first_ref, out_ref):
    blocks, pair, half, rows = first_ref.shape
    head = head_ref[0]
    for p in range(pair):
        block = first_ref[:, p].reshape(blocks * half, rows)
        y = dot(head, block, NT)
        n = blocks * half // rows
        for x in range(n):
            out_ref[p * n + x] = y[:, x * rows : (x + 1) * rows]


def add_up(got_ref, out_ref):
    total = jnp.sum(got_ref[...], axis=0)
    for c in range(out_ref.shape[0]):
        out_ref[c] = total


def advance(base, at, diag_at, solved_ref, head_ref, rest_hbm, y_out, line_ref, diag_ref, sems):
    group, rows = y_out.shape[0], y_out.shape[2]
    first = pltpu.make_async_copy(rest_hbm.at[at], line_ref, sems.at[0])
    second = pltpu.make_async_copy(rest_hbm.at[diag_at], diag_ref, sems.at[1])
    first.start()
    second.start()
    x = chosen(solved_ref)
    first.wait()
    head = head_ref[base] - dot(x, line_ref[...], NN)
    second.wait()
    y = dot(head, diag_ref[...], NT)
    for s in range(group):
        y_out[s] = y[:, s * rows : (s + 1) * rows]


def chosen(solved_ref):
    return jnp.concatenate([solved_ref[s] for s in range(solved_ref.shape[0])], axis=1)


def follow(base, at, solved_ref, heads_ref, rest_hbm, heads_out, lines_ref, sem):
    left = heads_out.shape[0]
    copy = pltpu.make_async_copy(rest_hbm.at[pl.ds(at, left)], lines_ref, sem)
    copy.start()
    x = chosen(solved_ref)
    copy.wait()
    for b in range(left):
        heads_out[b] = heads_ref[base + b + 1] - dot(x, lines_ref[b], NN)


def stacked(x_refs):
    if len(x_refs) == 1:
        parts = [x_refs[0][s].reshape(-1, x_refs[0].shape[-1]) for s in range(2)]
    else:
        parts = [jnp.concatenate([x[0, s] for x in x_refs], axis=0) for s in range(2)]
    return jnp.concatenate(parts, axis=1)


def trail_sum(n, *refs):
    x_refs, f_ref, out_ref = refs[:n], refs[n], refs[-1]

    @pl.when(pl.program_id(0) == 0)
    def _():
        out_ref[...] = jnp.zeros_like(out_ref) if len(refs) == n + 2 else refs[n + 1][...]

    out_ref[...] += dot(stacked(x_refs), f_ref[0, 0], NN)


def finish(panel, x_ref, f_hbm, sum_ref, quad_ref, r_hbm, *refs):
    own_refs, (out_ref, mine_ref, turned_ref, f_ref, r_ref, sems) = refs[:-6], refs[-6:]
    n = f_ref.shape[0]
    copies = [
        pltpu.make_async_copy(f_hbm.at[panel, b], f_ref.at[b], sems.at[b]) for b in range(n)
    ]
    for c in copies:
        c.start()
    width = mine_ref.shape[0] // len(own_refs)
    rows = pltpu.make_async_copy(
        r_hbm.at[pl.ds(mine_ref.shape[0], r_ref.shape[0])], r_ref, sems.at[n]
    )
    rows.start()
    quad = quad_ref[0]
    quads, per, _ = own_refs[0].shape
    at = pl.multiple_of(quad * width, width)
    for k, own_ref in enumerate(own_refs):
        shift = quads - quad if k < panel else 0
        own = [own_ref[lax.rem(q + shift, quads)] for q in range(quads)]
        turned_ref[...] = jnp.concatenate(own, axis=0).T
        mine_ref[k * width : (k + 1) * width] = turned_ref[pl.ds(at, width)]
    total = jnp.concatenate(
        [
            sum_ref[pl.ds(pl.multiple_of(lax.rem(q + quads - quad, quads) * per, per), per)]
            for q in range(quads)
        ],
        axis=0,
    )
    for b, c in enumerate(copies):
        c.wait()
        total += dot(stacked([x_ref.at[pl.ds(2 * b, 2)]]), f_ref[b], NN)
    rows.wait()
    out_ref[...] = r_ref[...] - total.T


def trail_call(kernel, x, f, k, out_shape, extra=(), specs=(), steps=1, scratch=()):
    per_pair = f.shape[2] // 256
    per_panel = f.shape[1] * per_pair
    if len(x) == 1:
        x_specs = [pl.BlockSpec((2, *x[0].shape[1:]), lambda i: (i % per_panel, 0, 0, 0))]
    else:
        x_specs = [
            pl.BlockSpec((1, 2, *p.shape[2:]), lambda i: (i // per_panel, i % per_panel, 0, 0))
            for p in x
        ]
    f_spec = pl.BlockSpec(
        (1, 1, 256, f.shape[3]),
        lambda i: (k + i // per_panel, (i % per_panel) // per_pair, i % per_pair, 0),
    )
    return pl.pallas_call(
        kernel,
        out_shape=jax.ShapeDtypeStruct(out_shape, F32),
        grid=(steps * per_panel,),
        in_specs=[*x_specs, f_spec, *specs],
        out_specs=whole(out_shape),
        scratch_shapes=scratch,
        compiler_params=pltpu.CompilerParams(vmem_limit_bytes=16 << 20),
    )(*x, in_hbm(f), *extra)


def spread(array, axes):
    return lax.all_to_all(
        jnp.broadcast_to(array[None], (lax.axis_size(axes), *array.shape)), axes, 0, 0, tiled=True
    )


def body(factor, inverses, right_side):
    lower = jnp.transpose(factor[0], (1, 2, 0))
    inv = jnp.transpose(inverses[0], (0, 2, 1))
    current = right_side[0]
    panels, cols, _ = lower.shape
    width = inv.shape[1]
    count = current.shape[1]
    tail = panels * width
    quads = lax.axis_size("yq")
    nx, npair = lax.axis_size("x"), lax.axis_size("yp")
    blocks = lax.axis_size(RHS)
    group = nx * npair
    per = count // quads
    rows = quads * width
    half = cols // npair
    quad = lax.axis_index("yq")

    index = quad.reshape(1).astype(jnp.int32)
    (sent,) = call(
        pack,
        [(quads, per + 2 * cols + half, tail)],
        [HBM, HBM, HBM],
        [
            pltpu.VMEM((panels, cols, tail), F32),
            pltpu.VMEM(inv.shape, F32),
            pltpu.VMEM((tail, count), F32),
            pltpu.SemaphoreType.DMA((3,)),
        ],
    )(in_hbm(lower), in_hbm(inv), in_hbm(current))
    got = lax.all_to_all(sent, "yq", 0, 0, tiled=True)
    heads, pay, first = call(
        lambda *refs: sort(width, per, *refs),
        [(panels, per, rows), (9, npair, half, rows), (blocks, npair, half, rows)],
        [VMEM],
    )(got)
    first = lax.all_to_all(first, RHS, 0, 0, tiled=True)
    rest = lax.all_gather(pay, RHS, axis=2, tiled=True)
    rest = rest.reshape(9, group * rows, rows)

    (y,) = call(begin, [(group, per, rows)], [VMEM, VMEM])(heads, first)
    length = lower.shape[2] - tail
    place = lax.axis_index("yp") * nx + lax.axis_index("x")
    own, waiting, sent = {}, [], []
    trail = total = None
    for k in range(panels):
        got = lax.all_to_all(y, GROUP, 0, 0, tiled=True)
        copies = group if k < panels - 1 else quads
        (mine,) = call(add_up, [(copies, per, rows)], [VMEM])(got)
        if k == 0:
            lower, mine = lax.optimization_barrier((lower, mine))
            trail = lower[:, :, tail:].reshape(panels, npair, half, -1)
            trail = lax.all_gather(trail, RHS, axis=2, tiled=True)
        if k == panels - 1:
            mine = lax.all_to_all(mine, "yq", 0, 0, tiled=True)
            own[k] = mine
            solved = spread(mine, GROUP)
            break
        solved = lax.all_to_all(mine, GROUP, 0, 0, tiled=True)
        waiting.append(solved)
        if len(sent) < len(BATCHES) and BATCHES[len(sent)][-1] == k:
            batch = jnp.stack(waiting)
            parts = [batch] + [
                lax.ppermute(batch, "yq", [(i, (i - t) % quads) for i in range(quads)])
                for t in range(1, quads)
            ]
            sent.append(parts)
            waiting = []
        left = panels - 1 - k
        at = {3: 3, 2: 6, 1: 8}[left]
        one = pltpu.VMEM((group * rows, rows), F32)
        (y,) = call(
            lambda *refs, at=at, k=k: advance(int(k == 0), at, k, *refs),
            [(group, per, rows)],
            [VMEM, VMEM, HBM],
            [one, one, pltpu.SemaphoreType.DMA((2,))],
        )(solved, heads, in_hbm(rest))
        if left > 1:
            (heads,) = call(
                lambda *refs, at=at, k=k: follow(int(k == 0), at + 1, *refs),
                [(left - 1, per, rows)],
                [VMEM, VMEM, HBM],
                [
                    pltpu.VMEM((left - 1, group * rows, rows), F32),
                    pltpu.SemaphoreType.DMA,
                ],
            )(solved, heads, in_hbm(rest))

    for batch, parts in zip(BATCHES, sent):
        total = add_trail(parts, trail, batch[0], len(batch), total)
        here = [lax.dynamic_index_in_dim(p, place, 1, keepdims=False) for p in parts]
        for n, k in enumerate(batch):
            own[k] = jnp.stack([p[n] for p in here])
    flat = trail.reshape(panels, -1, 2 * rows, length)
    out, mine = call(
        lambda *refs: finish(panels - 1, *refs),
        [(length, count), (tail, count)],
        [VMEM, HBM, VMEM, SMEM, HBM] + [VMEM] * panels,
        [
            pltpu.VMEM((rows, count), F32),
            pltpu.VMEM(flat.shape[1:], F32),
            pltpu.VMEM((length, count), F32),
            pltpu.SemaphoreType.DMA((flat.shape[1] + 1,)),
        ],
    )(solved, in_hbm(flat), total, index, in_hbm(current), *[own[k] for k in range(panels)])
    return (mine[None], out[None])


def add_trail(parts, trail, k, steps, total):
    shape = (len(parts) * parts[0].shape[2], trail.shape[3])
    more = () if total is None else (total,)
    return trail_call(
        lambda *refs: trail_sum(len(parts), *refs), parts, trail, k, shape,
        more, (whole(shape),) * len(more), steps,
    )


def solution(mesh):
    nx, ny, nz, nc = SIZES(mesh)
    fine = Mesh(
        mesh.devices.reshape(nx, QUADS, ny // QUADS, nz, nc), ("x", "yq", "yp", "z", "core")
    )
    row = ("x", "yq", "yp")
    in_specs = (P(row, None, None, RHS), P(row, None, RHS, None), P(row, None, RHS))
    out_specs = (P(row, None, RHS), P(row, None, RHS))
    return jax.shard_map(body, mesh=fine, in_specs=in_specs, out_specs=out_specs, check_vma=False)


def SIZES(mesh):
    nrow, nrhs = mesh.shape["row"], mesh.shape["rhs"]
    return nrow // 8, 8, nrhs // 2, 2
```

```python
import jax
import jax.numpy as jnp
from jax import lax
from jax.experimental import pallas as pl
from jax.experimental.pallas import tpu as pltpu
from jax.sharding import Mesh, PartitionSpec as P

QUADS = 4
RHS = ("z", "core")
GROUP = ("yp", "x")
F32 = jnp.float32


def halves(value):
    high = value.astype(jnp.bfloat16)
    return high, (value - high.astype(F32)).astype(jnp.bfloat16)


def dot(a, b, dims):
    def one(u, v):
        return lax.dot_general(u, v, (dims, ((), ())), preferred_element_type=F32)

    ah, al = halves(a)
    bh, bl = halves(b)
    return one(ah, bh) + (one(ah, bl) + one(al, bh))


NN = ((1,), (0,))
NT = ((1,), (1,))


VMEM = pl.BlockSpec(memory_space=pltpu.VMEM)
SMEM = pl.BlockSpec(memory_space=pltpu.SMEM)
HBM = pl.BlockSpec(memory_space=pltpu.HBM)


def call(kernel, shapes, in_specs, scratch=()):
    return pl.pallas_call(
        kernel,
        out_shape=[jax.ShapeDtypeStruct(s, F32) for s in shapes],
        in_specs=in_specs,
        out_specs=[VMEM] * len(shapes),
        scratch_shapes=scratch,
        compiler_params=pltpu.CompilerParams(vmem_limit_bytes=20 << 20),
    )


def in_hbm(array):
    return pltpu.with_memory_space_constraint(array, pltpu.HBM)


def whole(shape):
    return pl.BlockSpec(shape, lambda i: (0,) * len(shape))


def pack(f_hbm, inv_hbm, r_hbm, out_ref, f_ref, inv_ref, r_ref, sems):
    quads, _, lanes = out_ref.shape
    copies = [
        pltpu.make_async_copy(f_hbm.at[:, :, pl.ds(0, lanes)], f_ref, sems.at[0]),
        pltpu.make_async_copy(inv_hbm, inv_ref, sems.at[1]),
        pltpu.make_async_copy(r_hbm.at[pl.ds(0, lanes)], r_ref, sems.at[2]),
    ]
    for c in copies:
        c.start()
    for c in copies:
        c.wait()
    cols = f_ref.shape[1]
    per = r_ref.shape[1] // quads
    w = inv_ref.shape[1]
    turned = r_ref[...].T
    wide = jnp.concatenate([f_ref[0][:, w:], f_ref[2][:, 3 * w :]], axis=1)
    mid = f_ref[1][:, 2 * w :]
    mid = jnp.concatenate([mid[: cols // 2], mid[cols // 2 :]], axis=1)
    diag = jnp.concatenate([inv_ref[k].T for k in range(4)], axis=1)
    for q in range(quads):
        out_ref[q, :per] = turned[q * per : (q + 1) * per]
        out_ref[q, per : per + cols] = wide
        out_ref[q, per + cols : per + cols + cols // 2] = mid
        out_ref[q, per + cols + cols // 2 :] = diag


def sort(w, per, got_ref, heads_ref, pay_ref, first_ref):
    quads = got_ref.shape[0]
    half = pay_ref.shape[2]
    cols = 2 * half
    a, b, d = per, per + cols, per + cols + half

    def lanes(start, n, at):
        return jnp.concatenate(
            [got_ref[q, start : start + n][:, at : at + w] for q in range(quads)], axis=1
        )

    for k in range(4):
        heads_ref[k] = lanes(0, per, k * w)
    for h in range(2):
        for k in range(1, 4):
            pay_ref[k - 1, h] = lanes(d + h * half, half, k * w)
        for j in range(3):
            pay_ref[3 + j, h] = lanes(a + h * half, half, j * w)
        for j in range(2):
            pay_ref[6 + j, h] = lanes(b, half, h * 2 * w + j * w)
        pay_ref[8, h] = lanes(a + h * half, half, 3 * w)
        piece = lanes(d + h * half, half, 0)
        for c in range(first_ref.shape[0]):
            first_ref[c, h] = piece


def begin(head_ref, first_ref, out_ref):
    blocks, pair, half, rows = first_ref.shape
    head = head_ref[0]
    for p in range(pair):
        block = first_ref[:, p].reshape(blocks * half, rows)
        y = dot(head, block, NT)
        n = blocks * half // rows
        for x in range(n):
            out_ref[p * n + x] = y[:, x * rows : (x + 1) * rows]


def add_up(got_ref, out_ref):
    total = jnp.sum(got_ref[...], axis=0)
    for c in range(out_ref.shape[0]):
        out_ref[c] = total


def advance(base, at, diag_at, solved_ref, head_ref, rest_hbm, y_out, line_ref, diag_ref, sems):
    group, rows = y_out.shape[0], y_out.shape[2]
    first = pltpu.make_async_copy(rest_hbm.at[at], line_ref, sems.at[0])
    second = pltpu.make_async_copy(rest_hbm.at[diag_at], diag_ref, sems.at[1])
    first.start()
    second.start()
    x = chosen(solved_ref)
    first.wait()
    head = head_ref[base] - dot(x, line_ref[...], NN)
    second.wait()
    y = dot(head, diag_ref[...], NT)
    for s in range(group):
        y_out[s] = y[:, s * rows : (s + 1) * rows]


def chosen(solved_ref):
    return jnp.concatenate([solved_ref[s] for s in range(solved_ref.shape[0])], axis=1)


def follow(base, at, solved_ref, heads_ref, rest_hbm, heads_out, lines_ref, sem):
    left = heads_out.shape[0]
    copy = pltpu.make_async_copy(rest_hbm.at[pl.ds(at, left)], lines_ref, sem)
    copy.start()
    x = chosen(solved_ref)
    copy.wait()
    for b in range(left):
        heads_out[b] = heads_ref[base + b + 1] - dot(x, lines_ref[b], NN)


def others(quad_ref, got_ref, out_ref):
    copies, panels, turns = out_ref.shape[:3]
    quads = got_ref.shape[0]
    for t in range(turns):
        q = lax.rem(quad_ref[0] + (t + 1), quads)
        for k in range(panels):
            block = got_ref[q, k]
            for c in range(copies):
                out_ref[c, k, t] = block


def last_copies(panel, got_ref, out_ref):
    for c in range(out_ref.shape[0]):
        for q in range(got_ref.shape[0]):
            out_ref[c, q] = got_ref[q, panel]


def trail_sum(own_ref, x_ref, f_ref, out_ref):
    @pl.when(pl.program_id(0) == 0)
    def _():
        out_ref[...] = jnp.zeros_like(out_ref)

    parts = []
    for s in range(2):
        turns = [x_ref[s, 0, t] for t in range(x_ref.shape[2])]
        parts.append(jnp.concatenate([own_ref[0, s], *turns], axis=0))
    out_ref[...] += dot(jnp.concatenate(parts, axis=1), f_ref[0, 0], NN)


def finish(panel, x_ref, f_hbm, sum_ref, quad_ref, r_hbm, own_ref, *refs):
    out_ref, mine_ref, turned_ref, f_ref, r_ref, sems = refs
    n = f_ref.shape[0]
    copies = [
        pltpu.make_async_copy(f_hbm.at[panel, b], f_ref.at[b], sems.at[b]) for b in range(n)
    ]
    for c in copies:
        c.start()
    quads, panels, per, _ = own_ref.shape
    width = mine_ref.shape[0] // panels
    rows = pltpu.make_async_copy(
        r_hbm.at[pl.ds(mine_ref.shape[0], r_ref.shape[0])], r_ref, sems.at[n]
    )
    rows.start()
    quad = quad_ref[0]
    at = pl.multiple_of(quad * width, width)
    for k in range(panels):
        turned_ref[...] = jnp.concatenate([own_ref[q, k] for q in range(quads)], axis=0).T
        mine_ref[k * width : (k + 1) * width] = turned_ref[pl.ds(at, width)]
    total = jnp.concatenate(
        [
            sum_ref[pl.ds(pl.multiple_of(lax.rem(q + quads - quad, quads) * per, per), per)]
            for q in range(quads)
        ],
        axis=0,
    )
    for b, c in enumerate(copies):
        c.wait()
        x = [x_ref[2 * b + s].reshape(-1, x_ref.shape[3]) for s in range(2)]
        total += dot(jnp.concatenate(x, axis=1), f_ref[b], NN)
    rows.wait()
    out_ref[...] = r_ref[...] - total.T


def spread(array, axes):
    return lax.all_to_all(
        jnp.broadcast_to(array[None], (lax.axis_size(axes), *array.shape)), axes, 0, 0, tiled=True
    )


def body(factor, inverses, right_side):
    lower = jnp.transpose(factor[0], (1, 2, 0))
    inv = jnp.transpose(inverses[0], (0, 2, 1))
    current = right_side[0]
    panels, cols, _ = lower.shape
    width = inv.shape[1]
    count = current.shape[1]
    tail = panels * width
    quads = lax.axis_size("yq")
    nx, npair = lax.axis_size("x"), lax.axis_size("yp")
    blocks = lax.axis_size(RHS)
    group = nx * npair
    per = count // quads
    rows = quads * width
    half = cols // npair
    quad = lax.axis_index("yq")

    index = quad.reshape(1).astype(jnp.int32)
    (sent,) = call(
        pack,
        [(quads, per + 2 * cols + half, tail)],
        [HBM, HBM, HBM],
        [
            pltpu.VMEM((panels, cols, tail), F32),
            pltpu.VMEM(inv.shape, F32),
            pltpu.VMEM((tail, count), F32),
            pltpu.SemaphoreType.DMA((3,)),
        ],
    )(in_hbm(lower), in_hbm(inv), in_hbm(current))
    got = lax.all_to_all(sent, "yq", 0, 0, tiled=True)
    heads, pay, first = call(
        lambda *refs: sort(width, per, *refs),
        [(panels, per, rows), (9, npair, half, rows), (blocks, npair, half, rows)],
        [VMEM],
    )(got)
    first = lax.all_to_all(first, RHS, 0, 0, tiled=True)
    rest = lax.all_gather(pay, RHS, axis=2, tiled=True)
    trail = lower[:, :, tail:].reshape(panels, npair, half, -1)
    trail = lax.all_gather(trail, RHS, axis=2, tiled=True)
    rest = rest.reshape(9, group * rows, rows)

    (y,) = call(begin, [(group, per, rows)], [VMEM, VMEM])(heads, first)
    length = lower.shape[2] - tail
    mine, solved = [], []
    for k in range(panels):
        got = lax.all_to_all(y, GROUP, 0, 0, tiled=True)
        copies = group if k < panels - 1 else 1
        (copied,) = call(add_up, [(copies, per, rows)], [VMEM])(got)
        mine.append(copied[0])
        if k == panels - 1:
            break
        solved.append(lax.all_to_all(copied, GROUP, 0, 0, tiled=True))
        left = panels - 1 - k
        at = {3: 3, 2: 6, 1: 8}[left]
        one = pltpu.VMEM((group * rows, rows), F32)
        (y,) = call(
            lambda *refs, at=at, k=k: advance(int(k == 0), at, k, *refs),
            [(group, per, rows)],
            [VMEM, VMEM, HBM],
            [one, one, pltpu.SemaphoreType.DMA((2,))],
        )(solved[k], heads, in_hbm(rest))
        if left > 1:
            (heads,) = call(
                lambda *refs, at=at, k=k: follow(int(k == 0), at + 1, *refs),
                [(left - 1, per, rows)],
                [VMEM, VMEM, HBM],
                [
                    pltpu.VMEM((left - 1, group * rows, rows), F32),
                    pltpu.SemaphoreType.DMA,
                ],
            )(solved[k], heads, in_hbm(rest))

    own = spread(jnp.stack(mine), "yq")
    (sent,) = call(others, [(group, panels - 1, quads - 1, per, rows)], [SMEM, VMEM])(index, own)
    early = lax.all_to_all(sent, GROUP, 0, 0, tiled=True)
    own, early = lax.optimization_barrier((own, early))
    (sent,) = call(lambda *refs: last_copies(panels - 1, *refs), [(group, quads, per, rows)], [VMEM])(own)
    late = lax.all_to_all(sent, GROUP, 0, 0, tiled=True)

    per_pair = trail.shape[2] // (2 * rows)
    per_panel = npair * per_pair
    total = pl.pallas_call(
        trail_sum,
        out_shape=jax.ShapeDtypeStruct((count, length), F32),
        grid=((panels - 1) * per_panel,),
        in_specs=[
            pl.BlockSpec((1, 2, per, rows), lambda i: (i // per_panel, i % per_panel, 0, 0)),
            pl.BlockSpec(
                (2, 1, quads - 1, per, rows), lambda i: (i % per_panel, i // per_panel, 0, 0, 0)
            ),
            pl.BlockSpec(
                (1, 1, 2 * rows, length),
                lambda i: (i // per_panel, (i % per_panel) // per_pair, i % per_pair, 0),
            ),
        ],
        out_specs=whole((count, length)),
        compiler_params=pltpu.CompilerParams(vmem_limit_bytes=16 << 20),
    )(in_hbm(jnp.stack(solved)), early, in_hbm(trail))
    flat = trail.reshape(panels, -1, 2 * rows, length)
    out, mine = call(
        lambda *refs: finish(panels - 1, *refs),
        [(length, count), (tail, count)],
        [VMEM, HBM, VMEM, SMEM, HBM, VMEM],
        [
            pltpu.VMEM((rows, count), F32),
            pltpu.VMEM(flat.shape[1:], F32),
            pltpu.VMEM((length, count), F32),
            pltpu.SemaphoreType.DMA((flat.shape[1] + 1,)),
        ],
    )(late, in_hbm(flat), total, index, in_hbm(current), own)
    return (mine[None], out[None])


def solution(mesh):
    nx, ny, nz, nc = SIZES(mesh)
    fine = Mesh(
        mesh.devices.reshape(nx, QUADS, ny // QUADS, nz, nc), ("x", "yq", "yp", "z", "core")
    )
    row = ("x", "yq", "yp")
    in_specs = (P(row, None, None, RHS), P(row, None, RHS, None), P(row, None, RHS))
    out_specs = (P(row, None, RHS), P(row, None, RHS))
    return jax.shard_map(body, mesh=fine, in_specs=in_specs, out_specs=out_specs, check_vma=False)


def SIZES(mesh):
    nrow, nrhs = mesh.shape["row"], mesh.shape["rhs"]
    return nrow // 8, 8, nrhs // 2, 2
```

```python
import jax
import jax.numpy as jnp
from jax import lax
from jax.experimental import pallas as pl
from jax.experimental.pallas import tpu as pltpu
from jax.sharding import Mesh, PartitionSpec as P

QUADS = 4
RHS = ("z", "core")
GROUP = ("yp", "x")
F32 = jnp.float32


def halves(value):
    high = value.astype(jnp.bfloat16)
    return high, (value - high.astype(F32)).astype(jnp.bfloat16)


def dot(a, b, dims):
    def one(u, v):
        return lax.dot_general(u, v, (dims, ((), ())), preferred_element_type=F32)

    ah, al = halves(a)
    bh, bl = halves(b)
    return one(ah, bh) + (one(ah, bl) + one(al, bh))


NN = ((1,), (0,))
NT = ((1,), (1,))


VMEM = pl.BlockSpec(memory_space=pltpu.VMEM)
SMEM = pl.BlockSpec(memory_space=pltpu.SMEM)
HBM = pl.BlockSpec(memory_space=pltpu.HBM)


def call(kernel, shapes, in_specs, scratch=()):
    return pl.pallas_call(
        kernel,
        out_shape=[jax.ShapeDtypeStruct(s, F32) for s in shapes],
        in_specs=in_specs,
        out_specs=[VMEM] * len(shapes),
        scratch_shapes=scratch,
        compiler_params=pltpu.CompilerParams(vmem_limit_bytes=20 << 20),
    )


def in_hbm(array):
    return pltpu.with_memory_space_constraint(array, pltpu.HBM)


def whole(shape):
    return pl.BlockSpec(shape, lambda i: (0,) * len(shape))


def pack(f_hbm, inv_hbm, r_hbm, out_ref, f_ref, inv_ref, r_ref, sems):
    quads, _, lanes = out_ref.shape
    copies = [
        pltpu.make_async_copy(f_hbm.at[:, :, pl.ds(0, lanes)], f_ref, sems.at[0]),
        pltpu.make_async_copy(inv_hbm, inv_ref, sems.at[1]),
        pltpu.make_async_copy(r_hbm.at[pl.ds(0, lanes)], r_ref, sems.at[2]),
    ]
    for c in copies:
        c.start()
    for c in copies:
        c.wait()
    cols = f_ref.shape[1]
    per = r_ref.shape[1] // quads
    w = inv_ref.shape[1]
    turned = r_ref[...].T
    wide = jnp.concatenate([f_ref[0][:, w:], f_ref[2][:, 3 * w :]], axis=1)
    mid = f_ref[1][:, 2 * w :]
    mid = jnp.concatenate([mid[: cols // 2], mid[cols // 2 :]], axis=1)
    diag = jnp.concatenate([inv_ref[k].T for k in range(4)], axis=1)
    for q in range(quads):
        out_ref[q, :per] = turned[q * per : (q + 1) * per]
        out_ref[q, per : per + cols] = wide
        out_ref[q, per + cols : per + cols + cols // 2] = mid
        out_ref[q, per + cols + cols // 2 :] = diag


def sort(w, per, got_ref, heads_ref, pay_ref, first_ref):
    quads = got_ref.shape[0]
    half = pay_ref.shape[2]
    cols = 2 * half
    a, b, d = per, per + cols, per + cols + half

    def lanes(start, n, at):
        return jnp.concatenate(
            [got_ref[q, start : start + n][:, at : at + w] for q in range(quads)], axis=1
        )

    for k in range(4):
        heads_ref[k] = lanes(0, per, k * w)
    for h in range(2):
        for k in range(1, 4):
            pay_ref[k - 1, h] = lanes(d + h * half, half, k * w)
        for j in range(3):
            pay_ref[3 + j, h] = lanes(a + h * half, half, j * w)
        for j in range(2):
            pay_ref[6 + j, h] = lanes(b, half, h * 2 * w + j * w)
        pay_ref[8, h] = lanes(a + h * half, half, 3 * w)
        piece = lanes(d + h * half, half, 0)
        for c in range(first_ref.shape[0]):
            first_ref[c, h] = piece


def begin(core_ref, head_ref, mine_ref, other_ref, out_ref):
    n, pair, half, rows = mine_ref.shape
    head = head_ref[0]
    even = core_ref[0] == 0
    for p in range(pair):
        mine, other = mine_ref[:, p], other_ref[:, p]
        low = jnp.where(even, mine, other)
        high = jnp.where(even, other, mine)
        block = jnp.concatenate([low[:, None], high[:, None]], axis=1)
        y = dot(head, block.reshape(2 * n * half, rows), NT)
        m = 2 * n * half // rows
        for x in range(m):
            out_ref[p * m + x] = y[:, x * rows : (x + 1) * rows]


def add_all(got_ref, *refs):
    mine_refs, out_ref = refs[:-1], refs[-1]
    total = jnp.sum(got_ref[...], axis=0)
    for c in range(out_ref.shape[0]):
        for k, mine_ref in enumerate(mine_refs):
            out_ref[c, k] = mine_ref[...]
        out_ref[c, len(mine_refs)] = total


def add_up(got_ref, out_ref, mine_ref):
    total = jnp.sum(got_ref[...], axis=0)
    mine_ref[...] = total
    for c in range(out_ref.shape[0]):
        out_ref[c] = total


def advance(base, at, diag_at, solved_ref, head_ref, rest_hbm, y_out, line_ref, diag_ref, sems):
    group, rows = y_out.shape[0], y_out.shape[2]
    first = pltpu.make_async_copy(rest_hbm.at[at], line_ref, sems.at[0])
    second = pltpu.make_async_copy(rest_hbm.at[diag_at], diag_ref, sems.at[1])
    first.start()
    second.start()
    x = chosen(solved_ref)
    first.wait()
    head = head_ref[base] - dot(x, line_ref[...], NN)
    second.wait()
    y = dot(head, diag_ref[...], NT)
    for s in range(group):
        y_out[s] = y[:, s * rows : (s + 1) * rows]


def chosen(solved_ref):
    return jnp.concatenate([solved_ref[s] for s in range(solved_ref.shape[0])], axis=1)


def follow(base, at, solved_ref, heads_ref, rest_hbm, heads_out, lines_ref, sem):
    left = heads_out.shape[0]
    copy = pltpu.make_async_copy(rest_hbm.at[pl.ds(at, left)], lines_ref, sem)
    copy.start()
    x = chosen(solved_ref)
    copy.wait()
    for b in range(left):
        heads_out[b] = heads_ref[base + b + 1] - dot(x, lines_ref[b], NN)


def others(quad_ref, got_ref, out_ref):
    copies, panels, turns = out_ref.shape[:3]
    quads = got_ref.shape[0]
    for t in range(turns):
        q = lax.rem(quad_ref[0] + (t + 1), quads)
        for k in range(panels):
            block = got_ref[q, k]
            for c in range(copies):
                out_ref[c, k, t] = block


def last_copies(panel, got_ref, out_ref):
    for c in range(out_ref.shape[0]):
        for q in range(got_ref.shape[0]):
            out_ref[c, q] = got_ref[q, panel]


def trail_sum(steps, *refs):
    own_refs, (x_ref, f_ref, out_ref) = refs[:-3], refs[-3:]
    step = pl.program_id(0)

    @pl.when(step == 0)
    def _():
        out_ref[...] = jnp.zeros_like(out_ref)

    for k, own_ref in enumerate(own_refs):

        @pl.when(step // steps == k)
        def _():
            parts = []
            for s in range(2):
                turns = [x_ref[s, 0, t] for t in range(x_ref.shape[2])]
                parts.append(jnp.concatenate([own_ref[2 * (step % steps) + s], *turns], axis=0))
            out_ref[...] += dot(jnp.concatenate(parts, axis=1), f_ref[0, 0], NN)


def finish(panel, x_hbm, f_hbm, sum_hbm, quad_ref, r_hbm, own_ref, *refs):
    out_ref, mine_ref, turned_ref, f_ref, x_ref, sum_ref, r_ref, sems = refs
    n = f_ref.shape[0]
    quads, panels, per, _ = own_ref.shape
    width = mine_ref.shape[0] // panels
    copies = []
    for b in range(n):
        pair = pl.ds(2 * b, 2)
        copies += [
            pltpu.make_async_copy(x_hbm.at[pair], x_ref.at[pair], sems.at[2 * b]),
            pltpu.make_async_copy(f_hbm.at[panel, b], f_ref.at[b], sems.at[2 * b + 1]),
        ]
    sums = pltpu.make_async_copy(sum_hbm, sum_ref, sems.at[2 * n])
    rows = pltpu.make_async_copy(
        r_hbm.at[pl.ds(mine_ref.shape[0], r_ref.shape[0])], r_ref, sems.at[2 * n + 1]
    )
    for c in (*copies, sums, rows):
        c.start()
    quad = quad_ref[0]
    at = pl.multiple_of(quad * width, width)
    for k in range(panels):
        turned_ref[...] = jnp.concatenate([own_ref[q, k] for q in range(quads)], axis=0).T
        mine_ref[k * width : (k + 1) * width] = turned_ref[pl.ds(at, width)]
    total = None
    for b in range(n):
        copies[2 * b].wait()
        copies[2 * b + 1].wait()
        x = [x_ref[2 * b + s].reshape(-1, x_ref.shape[3]) for s in range(2)]
        product = dot(jnp.concatenate(x, axis=1), f_ref[b], NN)
        total = product if b == 0 else total + product
    sums.wait()
    total += jnp.concatenate(
        [
            sum_ref[pl.ds(pl.multiple_of(lax.rem(q + quads - quad, quads) * per, per), per)]
            for q in range(quads)
        ],
        axis=0,
    )
    rows.wait()
    out_ref[...] = r_ref[...] - total.T


def body(factor, inverses, right_side):
    lower = jnp.transpose(factor[0], (1, 2, 0))
    inv = jnp.transpose(inverses[0], (0, 2, 1))
    current = right_side[0]
    panels, cols, _ = lower.shape
    width = inv.shape[1]
    count = current.shape[1]
    tail = panels * width
    quads = lax.axis_size("yq")
    nx, npair = lax.axis_size("x"), lax.axis_size("yp")
    blocks = lax.axis_size(RHS)
    group = nx * npair
    per = count // quads
    rows = quads * width
    half = cols // npair
    quad = lax.axis_index("yq")

    index = quad.reshape(1).astype(jnp.int32)
    (sent,) = call(
        pack,
        [(quads, per + 2 * cols + half, tail)],
        [HBM, HBM, HBM],
        [
            pltpu.VMEM((panels, cols, tail), F32),
            pltpu.VMEM(inv.shape, F32),
            pltpu.VMEM((tail, count), F32),
            pltpu.SemaphoreType.DMA((3,)),
        ],
    )(in_hbm(lower), in_hbm(inv), in_hbm(current))
    got = lax.all_to_all(sent, "yq", 0, 0, tiled=True)
    trail = lower[:, :, tail:].reshape(panels, npair, half, -1)
    got, trail = lax.optimization_barrier((got, trail))
    heads, pay, first = call(
        lambda *refs: sort(width, per, *refs),
        [(panels, per, rows), (9, npair, half, rows), (blocks // 2, npair, half, rows)],
        [VMEM],
    )(got)
    first = lax.all_to_all(first, "z", 0, 0, tiled=True)
    other = lax.ppermute(first, "core", [(0, 1), (1, 0)])
    core = lax.axis_index("core").reshape(1).astype(jnp.int32)
    rest = lax.all_gather(pay, RHS, axis=2, tiled=True)
    trail = lax.all_gather(trail, RHS, axis=2, tiled=True)
    rest = rest.reshape(9, group * rows, rows)

    (y,) = call(begin, [(group, per, rows)], [SMEM, VMEM, VMEM, VMEM])(core, heads, first, other)
    length = lower.shape[2] - tail
    mine, solved = [], []
    for k in range(panels):
        got = lax.all_to_all(y, GROUP, 0, 0, tiled=True)
        if k == panels - 1:
            break
        copied, single = call(add_up, [(group, per, rows), (per, rows)], [VMEM])(got)
        mine.append(single)
        solved.append(lax.all_to_all(copied, GROUP, 0, 0, tiled=True))
        left = panels - 1 - k
        at = {3: 3, 2: 6, 1: 8}[left]
        one = pltpu.VMEM((group * rows, rows), F32)
        (y,) = call(
            lambda *refs, at=at, k=k: advance(int(k == 0), at, k, *refs),
            [(group, per, rows)],
            [VMEM, VMEM, HBM],
            [one, one, pltpu.SemaphoreType.DMA((2,))],
        )(solved[k], heads, in_hbm(rest))
        if left > 1:
            (heads,) = call(
                lambda *refs, at=at, k=k: follow(int(k == 0), at + 1, *refs),
                [(left - 1, per, rows)],
                [VMEM, VMEM, HBM],
                [
                    pltpu.VMEM((left - 1, group * rows, rows), F32),
                    pltpu.SemaphoreType.DMA,
                ],
            )(solved[k], heads, in_hbm(rest))

    (sent,) = call(add_all, [(quads, panels, per, rows)], [VMEM] * panels)(got, *mine)
    own = lax.all_to_all(sent, "yq", 0, 0, tiled=True)
    (sent,) = call(others, [(group, panels - 1, quads - 1, per, rows)], [SMEM, VMEM])(index, own)
    early = lax.all_to_all(sent, GROUP, 0, 0, tiled=True)
    own, early = lax.optimization_barrier((own, early))
    (sent,) = call(lambda *refs: last_copies(panels - 1, *refs), [(group, quads, per, rows)], [VMEM])(own)
    late = lax.all_to_all(sent, GROUP, 0, 0, tiled=True)

    per_pair = trail.shape[2] // (2 * rows)
    per_panel = npair * per_pair
    total = pl.pallas_call(
        lambda *refs: trail_sum(per_panel, *refs),
        out_shape=jax.ShapeDtypeStruct((count, length), F32),
        grid=((panels - 1) * per_panel,),
        in_specs=[
            *[whole((group, per, rows))] * (panels - 1),
            pl.BlockSpec(
                (2, 1, quads - 1, per, rows), lambda i: (i % per_panel, i // per_panel, 0, 0, 0)
            ),
            pl.BlockSpec(
                (1, 1, 2 * rows, length),
                lambda i: (i // per_panel, (i % per_panel) // per_pair, i % per_pair, 0),
            ),
        ],
        out_specs=whole((count, length)),
        compiler_params=pltpu.CompilerParams(vmem_limit_bytes=16 << 20),
    )(*solved, early, in_hbm(trail))
    flat = trail.reshape(panels, -1, 2 * rows, length)
    out, mine = call(
        lambda *refs: finish(panels - 1, *refs),
        [(length, count), (tail, count)],
        [HBM, HBM, HBM, SMEM, HBM, VMEM],
        [
            pltpu.VMEM((rows, count), F32),
            pltpu.VMEM(flat.shape[1:], F32),
            pltpu.VMEM(late.shape, F32),
            pltpu.VMEM(total.shape, F32),
            pltpu.VMEM((length, count), F32),
            pltpu.SemaphoreType.DMA((2 * flat.shape[1] + 2,)),
        ],
    )(in_hbm(late), in_hbm(flat), in_hbm(total), index, in_hbm(current), own)
    return (mine[None], out[None])


def solution(mesh):
    nx, ny, nz, nc = SIZES(mesh)
    fine = Mesh(
        mesh.devices.reshape(nx, QUADS, ny // QUADS, nz, nc), ("x", "yq", "yp", "z", "core")
    )
    row = ("x", "yq", "yp")
    in_specs = (P(row, None, None, RHS), P(row, None, RHS, None), P(row, None, RHS))
    out_specs = (P(row, None, RHS), P(row, None, RHS))
    return jax.shard_map(body, mesh=fine, in_specs=in_specs, out_specs=out_specs, check_vma=False)


def SIZES(mesh):
    nrow, nrhs = mesh.shape["row"], mesh.shape["rhs"]
    return nrow // 8, 8, nrhs // 2, 2
```

```python
import jax
import jax.numpy as jnp
from jax import lax
from jax.experimental import pallas as pl
from jax.experimental.pallas import tpu as pltpu
from jax.sharding import Mesh, PartitionSpec as P

QUADS = 4
RHS = ("z", "core")
GROUP = ("yp", "x")
F32 = jnp.float32


def halves(value):
    high = value.astype(jnp.bfloat16)
    return high, (value - high.astype(F32)).astype(jnp.bfloat16)


def dot(a, b, dims):
    def one(u, v):
        return lax.dot_general(u, v, (dims, ((), ())), preferred_element_type=F32)

    ah, al = halves(a)
    bh, bl = halves(b)
    return one(ah, bh) + (one(ah, bl) + one(al, bh))


NN = ((1,), (0,))
NT = ((1,), (1,))


VMEM = pl.BlockSpec(memory_space=pltpu.VMEM)
SMEM = pl.BlockSpec(memory_space=pltpu.SMEM)
HBM = pl.BlockSpec(memory_space=pltpu.HBM)


def call(kernel, shapes, in_specs, scratch=()):
    return pl.pallas_call(
        kernel,
        out_shape=[jax.ShapeDtypeStruct(s, F32) for s in shapes],
        in_specs=in_specs,
        out_specs=[VMEM] * len(shapes),
        scratch_shapes=scratch,
        compiler_params=pltpu.CompilerParams(vmem_limit_bytes=20 << 20),
    )


def in_hbm(array):
    return pltpu.with_memory_space_constraint(array, pltpu.HBM)


def whole(shape):
    return pl.BlockSpec(shape, lambda i: (0,) * len(shape))


def pack(f_hbm, inv_hbm, r_hbm, out_ref, f_ref, inv_ref, r_ref, sems):
    quads, _, lanes = out_ref.shape
    copies = [
        pltpu.make_async_copy(f_hbm.at[:, :, pl.ds(0, lanes)], f_ref, sems.at[0]),
        pltpu.make_async_copy(inv_hbm, inv_ref, sems.at[1]),
        pltpu.make_async_copy(r_hbm.at[pl.ds(0, lanes)], r_ref, sems.at[2]),
    ]
    for c in copies:
        c.start()
    for c in copies:
        c.wait()
    cols = f_ref.shape[1]
    per = r_ref.shape[1] // quads
    w = inv_ref.shape[1]
    turned = r_ref[...].T
    wide = jnp.concatenate([f_ref[0][:, w:], f_ref[2][:, 3 * w :]], axis=1)
    mid = f_ref[1][:, 2 * w :]
    mid = jnp.concatenate([mid[: cols // 2], mid[cols // 2 :]], axis=1)
    diag = jnp.concatenate([inv_ref[k].T for k in range(4)], axis=1)
    for q in range(quads):
        out_ref[q, :per] = turned[q * per : (q + 1) * per]
        out_ref[q, per : per + cols] = wide
        out_ref[q, per + cols : per + cols + cols // 2] = mid
        out_ref[q, per + cols + cols // 2 :] = diag


def sort(w, per, got_ref, heads_ref, pay_ref, first_ref):
    quads = got_ref.shape[0]
    half = pay_ref.shape[2]
    cols = 2 * half
    a, b, d = per, per + cols, per + cols + half

    def lanes(start, n, at):
        return jnp.concatenate(
            [got_ref[q, start : start + n][:, at : at + w] for q in range(quads)], axis=1
        )

    for k in range(4):
        heads_ref[k] = lanes(0, per, k * w)
    for h in range(2):
        for k in range(1, 4):
            pay_ref[k - 1, h] = lanes(d + h * half, half, k * w)
        for j in range(3):
            pay_ref[3 + j, h] = lanes(a + h * half, half, j * w)
        for j in range(2):
            pay_ref[6 + j, h] = lanes(b, half, h * 2 * w + j * w)
        pay_ref[8, h] = lanes(a + h * half, half, 3 * w)
        piece = lanes(d + h * half, half, 0)
        for c in range(first_ref.shape[0]):
            first_ref[c, h] = piece


def begin(core_ref, head_ref, mine_ref, other_ref, out_ref):
    n, pair, half, rows = mine_ref.shape
    head = head_ref[0]
    even = core_ref[0] == 0
    for p in range(pair):
        mine, other = mine_ref[:, p], other_ref[:, p]
        low = jnp.where(even, mine, other)
        high = jnp.where(even, other, mine)
        block = jnp.concatenate([low[:, None], high[:, None]], axis=1)
        y = dot(head, block.reshape(2 * n * half, rows), NT)
        m = 2 * n * half // rows
        for x in range(m):
            out_ref[p * m + x] = y[:, x * rows : (x + 1) * rows]


def add_all(got_ref, *refs):
    mine_refs, out_ref = refs[:-1], refs[-1]
    total = jnp.sum(got_ref[...], axis=0)
    for c in range(out_ref.shape[0]):
        for k, mine_ref in enumerate(mine_refs):
            out_ref[c, k] = mine_ref[...]
        out_ref[c, len(mine_refs)] = total


def add_up(got_ref, out_ref, mine_ref):
    total = jnp.sum(got_ref[...], axis=0)
    mine_ref[...] = total
    for c in range(out_ref.shape[0]):
        out_ref[c] = total


def advance(base, at, diag_at, solved_ref, head_ref, rest_hbm, y_out, line_ref, diag_ref, sems):
    group, rows = y_out.shape[0], y_out.shape[2]
    first = pltpu.make_async_copy(rest_hbm.at[at], line_ref, sems.at[0])
    second = pltpu.make_async_copy(rest_hbm.at[diag_at], diag_ref, sems.at[1])
    first.start()
    second.start()
    x = chosen(solved_ref)
    first.wait()
    head = head_ref[base] - dot(x, line_ref[...], NN)
    second.wait()
    y = dot(head, diag_ref[...], NT)
    for s in range(group):
        y_out[s] = y[:, s * rows : (s + 1) * rows]


def chosen(solved_ref):
    return jnp.concatenate([solved_ref[s] for s in range(solved_ref.shape[0])], axis=1)


def follow(base, at, solved_ref, heads_ref, rest_hbm, heads_out, lines_ref, sem):
    left = heads_out.shape[0]
    copy = pltpu.make_async_copy(rest_hbm.at[pl.ds(at, left)], lines_ref, sem)
    copy.start()
    x = chosen(solved_ref)
    copy.wait()
    for b in range(left):
        heads_out[b] = heads_ref[base + b + 1] - dot(x, lines_ref[b], NN)


def others(quad_ref, got_ref, out_ref):
    copies, panels, turns = out_ref.shape[:3]
    quads = got_ref.shape[0]
    for t in range(turns):
        q = lax.rem(quad_ref[0] + (t + 1), quads)
        for k in range(panels):
            block = got_ref[q, k]
            for c in range(copies):
                out_ref[c, k, t] = block


def last_copies(panel, got_ref, out_ref):
    for c in range(out_ref.shape[0]):
        for q in range(got_ref.shape[0]):
            out_ref[c, q] = got_ref[q, panel]


def trail_sum(steps, *refs):
    own_refs, (x_ref, f_ref, out_hbm, acc_ref, sem) = refs[:-5], refs[-5:]
    step = pl.program_id(0)

    @pl.when(step == 0)
    def _():
        acc_ref[...] = jnp.zeros_like(acc_ref)

    for k, own_ref in enumerate(own_refs):

        @pl.when(step // steps == k)
        def _():
            parts = []
            for s in range(2):
                turns = [x_ref[s, 0, t] for t in range(x_ref.shape[2])]
                parts.append(jnp.concatenate([own_ref[2 * (step % steps) + s], *turns], axis=0))
            acc_ref[...] += dot(jnp.concatenate(parts, axis=1), f_ref[0, 0], NN)

    @pl.when(step == pl.num_programs(0) - 1)
    def _():
        copy = pltpu.make_async_copy(acc_ref, out_hbm, sem)
        copy.start()
        copy.wait()


def finish(panel, x_hbm, f_hbm, sum_hbm, quad_ref, r_hbm, own_ref, *refs):
    out_ref, mine_ref, turned_ref, f_ref, x_ref, sum_ref, r_ref, sems = refs
    n = f_ref.shape[0]
    quads, panels, per, _ = own_ref.shape
    width = mine_ref.shape[0] // panels
    copies = []
    for b in range(n):
        pair = pl.ds(2 * b, 2)
        copies += [
            pltpu.make_async_copy(x_hbm.at[pair], x_ref.at[pair], sems.at[2 * b]),
            pltpu.make_async_copy(f_hbm.at[panel, b], f_ref.at[b], sems.at[2 * b + 1]),
        ]
    sums = pltpu.make_async_copy(sum_hbm, sum_ref, sems.at[2 * n])
    rows = pltpu.make_async_copy(
        r_hbm.at[pl.ds(mine_ref.shape[0], r_ref.shape[0])], r_ref, sems.at[2 * n + 1]
    )
    for c in (*copies, sums, rows):
        c.start()
    quad = quad_ref[0]
    at = pl.multiple_of(quad * width, width)
    for k in range(panels):
        turned_ref[...] = jnp.concatenate([own_ref[q, k] for q in range(quads)], axis=0).T
        mine_ref[k * width : (k + 1) * width] = turned_ref[pl.ds(at, width)]
    total = None
    for b in range(n):
        copies[2 * b].wait()
        copies[2 * b + 1].wait()
        x = [x_ref[2 * b + s].reshape(-1, x_ref.shape[3]) for s in range(2)]
        product = dot(jnp.concatenate(x, axis=1), f_ref[b], NN)
        total = product if b == 0 else total + product
    sums.wait()
    total += jnp.concatenate(
        [
            sum_ref[pl.ds(pl.multiple_of(lax.rem(q + quads - quad, quads) * per, per), per)]
            for q in range(quads)
        ],
        axis=0,
    )
    rows.wait()
    out_ref[...] = r_ref[...] - total.T


def body(factor, inverses, right_side):
    lower = jnp.transpose(factor[0], (1, 2, 0))
    inv = jnp.transpose(inverses[0], (0, 2, 1))
    current = right_side[0]
    panels, cols, _ = lower.shape
    width = inv.shape[1]
    count = current.shape[1]
    tail = panels * width
    quads = lax.axis_size("yq")
    nx, npair = lax.axis_size("x"), lax.axis_size("yp")
    blocks = lax.axis_size(RHS)
    group = nx * npair
    per = count // quads
    rows = quads * width
    half = cols // npair
    quad = lax.axis_index("yq")

    index = quad.reshape(1).astype(jnp.int32)
    (sent,) = call(
        pack,
        [(quads, per + 2 * cols + half, tail)],
        [HBM, HBM, HBM],
        [
            pltpu.VMEM((panels, cols, tail), F32),
            pltpu.VMEM(inv.shape, F32),
            pltpu.VMEM((tail, count), F32),
            pltpu.SemaphoreType.DMA((3,)),
        ],
    )(in_hbm(lower), in_hbm(inv), in_hbm(current))
    got = lax.all_to_all(sent, "yq", 0, 0, tiled=True)
    trail = lower[:, :, tail:].reshape(panels, npair, half, -1)
    core = lax.axis_index("core").reshape(1).astype(jnp.int32)
    got, trail, index, core = lax.optimization_barrier((got, trail, index, core))
    heads, pay, first = call(
        lambda *refs: sort(width, per, *refs),
        [(panels, per, rows), (9, npair, half, rows), (blocks // 2, npair, half, rows)],
        [VMEM],
    )(got)
    first = lax.all_to_all(first, "z", 0, 0, tiled=True)
    other = lax.ppermute(first, "core", [(0, 1), (1, 0)])
    rest = lax.all_gather(pay, RHS, axis=2, tiled=True)
    trail = lax.all_gather(trail, RHS, axis=2, tiled=True)
    rest = rest.reshape(9, group * rows, rows)

    (y,) = call(begin, [(group, per, rows)], [SMEM, VMEM, VMEM, VMEM])(core, heads, first, other)
    length = lower.shape[2] - tail
    mine, solved = [], []
    for k in range(panels):
        got = lax.all_to_all(y, GROUP, 0, 0, tiled=True)
        if k == panels - 1:
            break
        copied, single = call(add_up, [(group, per, rows), (per, rows)], [VMEM])(got)
        mine.append(single)
        solved.append(lax.all_to_all(copied, GROUP, 0, 0, tiled=True))
        left = panels - 1 - k
        at = {3: 3, 2: 6, 1: 8}[left]
        one = pltpu.VMEM((group * rows, rows), F32)
        (y,) = call(
            lambda *refs, at=at, k=k: advance(int(k == 0), at, k, *refs),
            [(group, per, rows)],
            [VMEM, VMEM, HBM],
            [one, one, pltpu.SemaphoreType.DMA((2,))],
        )(solved[k], heads, in_hbm(rest))
        if left > 1:
            (heads,) = call(
                lambda *refs, at=at, k=k: follow(int(k == 0), at + 1, *refs),
                [(left - 1, per, rows)],
                [VMEM, VMEM, HBM],
                [
                    pltpu.VMEM((left - 1, group * rows, rows), F32),
                    pltpu.SemaphoreType.DMA,
                ],
            )(solved[k], heads, in_hbm(rest))

    (sent,) = call(add_all, [(quads, panels, per, rows)], [VMEM] * panels)(got, *mine)
    own = lax.all_to_all(sent, "yq", 0, 0, tiled=True)
    (sent,) = call(others, [(group, panels - 1, quads - 1, per, rows)], [SMEM, VMEM])(index, own)
    early = lax.all_to_all(sent, GROUP, 0, 0, tiled=True)
    own, early = lax.optimization_barrier((own, early))
    (sent,) = call(lambda *refs: last_copies(panels - 1, *refs), [(group, quads, per, rows)], [VMEM])(own)
    late = lax.all_to_all(sent, GROUP, 0, 0, tiled=True)

    per_pair = trail.shape[2] // (2 * rows)
    per_panel = npair * per_pair
    total = pl.pallas_call(
        lambda *refs: trail_sum(per_panel, *refs),
        out_shape=pltpu.HBM((count, length), F32),
        grid=((panels - 1) * per_panel,),
        in_specs=[
            *[whole((group, per, rows))] * (panels - 1),
            pl.BlockSpec(
                (2, 1, quads - 1, per, rows), lambda i: (i % per_panel, i // per_panel, 0, 0, 0)
            ),
            pl.BlockSpec(
                (1, 1, 2 * rows, length),
                lambda i: (i // per_panel, (i % per_panel) // per_pair, i % per_pair, 0),
            ),
        ],
        out_specs=HBM,
        scratch_shapes=[pltpu.VMEM((count, length), F32), pltpu.SemaphoreType.DMA],
        compiler_params=pltpu.CompilerParams(vmem_limit_bytes=16 << 20),
    )(*[in_hbm(x) for x in solved], early, in_hbm(trail))
    flat = trail.reshape(panels, -1, 2 * rows, length)
    out, mine = call(
        lambda *refs: finish(panels - 1, *refs),
        [(length, count), (tail, count)],
        [HBM, HBM, HBM, SMEM, HBM, VMEM],
        [
            pltpu.VMEM((rows, count), F32),
            pltpu.VMEM(flat.shape[1:], F32),
            pltpu.VMEM(late.shape, F32),
            pltpu.VMEM(total.shape, F32),
            pltpu.VMEM((length, count), F32),
            pltpu.SemaphoreType.DMA((2 * flat.shape[1] + 2,)),
        ],
    )(in_hbm(late), in_hbm(flat), in_hbm(total), index, in_hbm(current), own)
    return (mine[None], out[None])


def solution(mesh):
    nx, ny, nz, nc = SIZES(mesh)
    fine = Mesh(
        mesh.devices.reshape(nx, QUADS, ny // QUADS, nz, nc), ("x", "yq", "yp", "z", "core")
    )
    row = ("x", "yq", "yp")
    in_specs = (P(row, None, None, RHS), P(row, None, RHS, None), P(row, None, RHS))
    out_specs = (P(row, None, RHS), P(row, None, RHS))
    return jax.shard_map(body, mesh=fine, in_specs=in_specs, out_specs=out_specs, check_vma=False)


def SIZES(mesh):
    nrow, nrhs = mesh.shape["row"], mesh.shape["rhs"]
    return nrow // 8, 8, nrhs // 2, 2
```

```python
import jax
import jax.numpy as jnp
from jax import lax
from jax.experimental import pallas as pl
from jax.experimental.pallas import tpu as pltpu
from jax.sharding import Mesh, PartitionSpec as P

QUADS = 4
RHS = ("z", "core")
GROUP = ("yp", "x")
F32 = jnp.float32


def halves(value):
    high = value.astype(jnp.bfloat16)
    return high, (value - high.astype(F32)).astype(jnp.bfloat16)


def dot(a, b, dims):
    def one(u, v):
        return lax.dot_general(u, v, (dims, ((), ())), preferred_element_type=F32)

    ah, al = halves(a)
    bh, bl = halves(b)
    return one(ah, bh) + (one(ah, bl) + one(al, bh))


NN = ((1,), (0,))
NT = ((1,), (1,))


VMEM = pl.BlockSpec(memory_space=pltpu.VMEM)
SMEM = pl.BlockSpec(memory_space=pltpu.SMEM)
HBM = pl.BlockSpec(memory_space=pltpu.HBM)


def call(kernel, shapes, in_specs, scratch=()):
    return pl.pallas_call(
        kernel,
        out_shape=[jax.ShapeDtypeStruct(s, F32) for s in shapes],
        in_specs=in_specs,
        out_specs=[VMEM] * len(shapes),
        scratch_shapes=scratch,
        compiler_params=pltpu.CompilerParams(vmem_limit_bytes=20 << 20),
    )


def in_hbm(array):
    return pltpu.with_memory_space_constraint(array, pltpu.HBM)


def whole(shape):
    return pl.BlockSpec(shape, lambda i: (0,) * len(shape))


def pack(f_hbm, inv_hbm, r_hbm, out_ref, f_ref, inv_ref, r_ref, sems):
    quads, _, lanes = out_ref.shape
    copies = [
        pltpu.make_async_copy(f_hbm.at[:, :, pl.ds(0, lanes)], f_ref, sems.at[0]),
        pltpu.make_async_copy(inv_hbm, inv_ref, sems.at[1]),
        pltpu.make_async_copy(r_hbm.at[pl.ds(0, lanes)], r_ref, sems.at[2]),
    ]
    for c in copies:
        c.start()
    for c in copies:
        c.wait()
    cols = f_ref.shape[1]
    per = r_ref.shape[1] // quads
    w = inv_ref.shape[1]
    turned = r_ref[...].T
    wide = jnp.concatenate([f_ref[0][:, w:], f_ref[2][:, 3 * w :]], axis=1)
    mid = f_ref[1][:, 2 * w :]
    mid = jnp.concatenate([mid[: cols // 2], mid[cols // 2 :]], axis=1)
    diag = jnp.concatenate([inv_ref[k].T for k in range(4)], axis=1)
    for q in range(quads):
        out_ref[q, :per] = turned[q * per : (q + 1) * per]
        out_ref[q, per : per + cols] = wide
        out_ref[q, per + cols : per + cols + cols // 2] = mid
        out_ref[q, per + cols + cols // 2 :] = diag


def sort(w, per, got_ref, heads_ref, soon_ref, later_ref, first_ref):
    quads = got_ref.shape[0]
    half = soon_ref.shape[2]
    cols = 2 * half
    a, b, d = per, per + cols, per + cols + half

    def lanes(start, n, at):
        return jnp.concatenate(
            [got_ref[q, start : start + n][:, at : at + w] for q in range(quads)], axis=1
        )

    for k in range(4):
        heads_ref[k] = lanes(0, per, k * w)
    for h in range(2):
        soon_ref[0, h] = lanes(d + h * half, half, w)
        soon_ref[1, h] = lanes(d + h * half, half, 2 * w)
        for j in range(3):
            soon_ref[2 + j, h] = lanes(a + h * half, half, j * w)
        soon_ref[5, h] = lanes(b, half, h * 2 * w)
        later_ref[0, h] = lanes(d + h * half, half, 3 * w)
        later_ref[1, h] = lanes(b, half, h * 2 * w + w)
        later_ref[2, h] = lanes(a + h * half, half, 3 * w)
        piece = lanes(d + h * half, half, 0)
        for c in range(first_ref.shape[0]):
            first_ref[c, h] = piece


def begin(core_ref, head_ref, mine_ref, other_ref, out_ref):
    n, pair, half, rows = mine_ref.shape
    head = head_ref[0]
    even = core_ref[0] == 0
    for p in range(pair):
        mine, other = mine_ref[:, p], other_ref[:, p]
        low = jnp.where(even, mine, other)
        high = jnp.where(even, other, mine)
        block = jnp.concatenate([low[:, None], high[:, None]], axis=1)
        y = dot(head, block.reshape(2 * n * half, rows), NT)
        m = 2 * n * half // rows
        for x in range(m):
            out_ref[p * m + x] = y[:, x * rows : (x + 1) * rows]


def add_all(got_ref, *refs):
    mine_refs, out_ref = refs[:-1], refs[-1]
    total = jnp.sum(got_ref[...], axis=0)
    for c in range(out_ref.shape[0]):
        for k, mine_ref in enumerate(mine_refs):
            out_ref[c, k] = mine_ref[...]
        out_ref[c, len(mine_refs)] = total


def add_up(got_ref, out_ref, mine_ref):
    total = jnp.sum(got_ref[...], axis=0)
    mine_ref[...] = total
    for c in range(out_ref.shape[0]):
        out_ref[c] = total


def advance(base, at, diag_at, solved_ref, head_ref, rest_hbm, y_out, line_ref, diag_ref, sems):
    group, rows = y_out.shape[0], y_out.shape[2]
    first = pltpu.make_async_copy(rest_hbm.at[at], line_ref, sems.at[0])
    second = pltpu.make_async_copy(rest_hbm.at[diag_at], diag_ref, sems.at[1])
    first.start()
    second.start()
    x = chosen(solved_ref)
    first.wait()
    head = head_ref[base] - dot(x, line_ref[...], NN)
    second.wait()
    y = dot(head, diag_ref[...], NT)
    for s in range(group):
        y_out[s] = y[:, s * rows : (s + 1) * rows]


def chosen(solved_ref):
    return jnp.concatenate([solved_ref[s] for s in range(solved_ref.shape[0])], axis=1)


def follow(base, at, solved_ref, heads_ref, rest_hbm, heads_out, lines_ref, sem):
    left = heads_out.shape[0]
    copy = pltpu.make_async_copy(rest_hbm.at[pl.ds(at, left)], lines_ref, sem)
    copy.start()
    x = chosen(solved_ref)
    copy.wait()
    for b in range(left):
        heads_out[b] = heads_ref[base + b + 1] - dot(x, lines_ref[b], NN)


def others(quad_ref, got_ref, out_ref):
    copies, panels, turns = out_ref.shape[:3]
    quads = got_ref.shape[0]
    for t in range(turns):
        q = lax.rem(quad_ref[0] + (t + 1), quads)
        for k in range(panels):
            block = got_ref[q, k]
            for c in range(copies):
                out_ref[c, k, t] = block


def last_copies(panel, got_ref, out_ref):
    for c in range(out_ref.shape[0]):
        for q in range(got_ref.shape[0]):
            out_ref[c, q] = got_ref[q, panel]


def trail_sum(steps, *refs):
    own_refs, (x_ref, f_ref, out_hbm, acc_ref, sem) = refs[:-5], refs[-5:]
    step = pl.program_id(0)

    @pl.when(step == 0)
    def _():
        acc_ref[...] = jnp.zeros_like(acc_ref)

    for k, own_ref in enumerate(own_refs):

        @pl.when(step // steps == k)
        def _():
            parts = []
            for s in range(2):
                turns = [x_ref[s, 0, t] for t in range(x_ref.shape[2])]
                parts.append(jnp.concatenate([own_ref[2 * (step % steps) + s], *turns], axis=0))
            acc_ref[...] += dot(jnp.concatenate(parts, axis=1), f_ref[0, 0], NN)

    @pl.when(step == pl.num_programs(0) - 1)
    def _():
        copy = pltpu.make_async_copy(acc_ref, out_hbm, sem)
        copy.start()
        copy.wait()


def finish(panel, x_hbm, f_hbm, sum_hbm, quad_ref, r_hbm, own_ref, *refs):
    out_ref, mine_ref, turned_ref, f_ref, x_ref, sum_ref, r_ref, sems = refs
    n = f_ref.shape[0]
    quads, panels, per, _ = own_ref.shape
    width = mine_ref.shape[0] // panels
    copies = []
    for b in range(n):
        pair = pl.ds(2 * b, 2)
        copies += [
            pltpu.make_async_copy(x_hbm.at[pair], x_ref.at[pair], sems.at[2 * b]),
            pltpu.make_async_copy(f_hbm.at[panel, b], f_ref.at[b], sems.at[2 * b + 1]),
        ]
    sums = pltpu.make_async_copy(sum_hbm, sum_ref, sems.at[2 * n])
    rows = pltpu.make_async_copy(
        r_hbm.at[pl.ds(mine_ref.shape[0], r_ref.shape[0])], r_ref, sems.at[2 * n + 1]
    )
    for c in (*copies, sums, rows):
        c.start()
    quad = quad_ref[0]
    at = pl.multiple_of(quad * width, width)
    for k in range(panels):
        turned_ref[...] = jnp.concatenate([own_ref[q, k] for q in range(quads)], axis=0).T
        mine_ref[k * width : (k + 1) * width] = turned_ref[pl.ds(at, width)]
    total = None
    for b in range(n):
        copies[2 * b].wait()
        copies[2 * b + 1].wait()
        x = [x_ref[2 * b + s].reshape(-1, x_ref.shape[3]) for s in range(2)]
        product = dot(jnp.concatenate(x, axis=1), f_ref[b], NN)
        total = product if b == 0 else total + product
    sums.wait()
    total += jnp.concatenate(
        [
            sum_ref[pl.ds(pl.multiple_of(lax.rem(q + quads - quad, quads) * per, per), per)]
            for q in range(quads)
        ],
        axis=0,
    )
    rows.wait()
    out_ref[...] = r_ref[...] - total.T


def body(factor, inverses, right_side):
    lower = jnp.transpose(factor[0], (1, 2, 0))
    inv = jnp.transpose(inverses[0], (0, 2, 1))
    current = right_side[0]
    panels, cols, _ = lower.shape
    width = inv.shape[1]
    count = current.shape[1]
    tail = panels * width
    quads = lax.axis_size("yq")
    nx, npair = lax.axis_size("x"), lax.axis_size("yp")
    blocks = lax.axis_size(RHS)
    group = nx * npair
    per = count // quads
    rows = quads * width
    half = cols // npair
    quad = lax.axis_index("yq")

    index = quad.reshape(1).astype(jnp.int32)
    (sent,) = call(
        pack,
        [(quads, per + 2 * cols + half, tail)],
        [HBM, HBM, HBM],
        [
            pltpu.VMEM((panels, cols, tail), F32),
            pltpu.VMEM(inv.shape, F32),
            pltpu.VMEM((tail, count), F32),
            pltpu.SemaphoreType.DMA((3,)),
        ],
    )(in_hbm(lower), in_hbm(inv), in_hbm(current))
    got = lax.all_to_all(sent, "yq", 0, 0, tiled=True)
    trail = lower[:, :, tail:].reshape(panels, npair, half, -1)
    core = lax.axis_index("core").reshape(1).astype(jnp.int32)
    got, trail, index, core = lax.optimization_barrier((got, trail, index, core))
    heads, soon, later, first = call(
        lambda *refs: sort(width, per, *refs),
        [
            (panels, per, rows),
            (6, npair, half, rows),
            (3, npair, half, rows),
            (blocks // 2, npair, half, rows),
        ],
        [VMEM],
    )(got)
    first = lax.all_to_all(first, "z", 0, 0, tiled=True)
    other = lax.ppermute(first, "core", [(0, 1), (1, 0)])
    soon = lax.all_gather(soon, RHS, axis=2, tiled=True)
    later = lax.all_gather(later, RHS, axis=2, tiled=True)
    trail = lax.all_gather(trail, RHS, axis=2, tiled=True)
    soon = soon.reshape(6, group * rows, rows)
    later = later.reshape(3, group * rows, rows)

    (y,) = call(begin, [(group, per, rows)], [SMEM, VMEM, VMEM, VMEM])(core, heads, first, other)
    length = lower.shape[2] - tail
    mine, solved = [], []
    for k in range(panels):
        got = lax.all_to_all(y, GROUP, 0, 0, tiled=True)
        if k == panels - 1:
            break
        copied, single = call(add_up, [(group, per, rows), (per, rows)], [VMEM])(got)
        mine.append(single)
        solved.append(lax.all_to_all(copied, GROUP, 0, 0, tiled=True))
        left = panels - 1 - k
        block, at, diag_at = ((soon, 2, 0), (soon, 5, 1), (later, 2, 0))[k]
        one = pltpu.VMEM((group * rows, rows), F32)
        (y,) = call(
            lambda *refs, at=at, diag_at=diag_at, k=k: advance(int(k == 0), at, diag_at, *refs),
            [(group, per, rows)],
            [VMEM, VMEM, HBM],
            [one, one, pltpu.SemaphoreType.DMA((2,))],
        )(solved[k], heads, in_hbm(block))
        if left > 1:
            (heads,) = call(
                lambda *refs, k=k: follow(int(k == 0), (3, 1)[k], *refs),
                [(left - 1, per, rows)],
                [VMEM, VMEM, HBM],
                [
                    pltpu.VMEM((left - 1, group * rows, rows), F32),
                    pltpu.SemaphoreType.DMA,
                ],
            )(solved[k], heads, in_hbm((soon, later)[k]))

    (sent,) = call(add_all, [(quads, panels, per, rows)], [VMEM] * panels)(got, *mine)
    own = lax.all_to_all(sent, "yq", 0, 0, tiled=True)
    (sent,) = call(others, [(group, panels - 1, quads - 1, per, rows)], [SMEM, VMEM])(index, own)
    early = lax.all_to_all(sent, GROUP, 0, 0, tiled=True)
    own, early = lax.optimization_barrier((own, early))
    (sent,) = call(lambda *refs: last_copies(panels - 1, *refs), [(group, quads, per, rows)], [VMEM])(own)
    late = lax.all_to_all(sent, GROUP, 0, 0, tiled=True)

    per_pair = trail.shape[2] // (2 * rows)
    per_panel = npair * per_pair
    total = pl.pallas_call(
        lambda *refs: trail_sum(per_panel, *refs),
        out_shape=pltpu.HBM((count, length), F32),
        grid=((panels - 1) * per_panel,),
        in_specs=[
            *[whole((group, per, rows))] * (panels - 1),
            pl.BlockSpec(
                (2, 1, quads - 1, per, rows), lambda i: (i % per_panel, i // per_panel, 0, 0, 0)
            ),
            pl.BlockSpec(
                (1, 1, 2 * rows, length),
                lambda i: (i // per_panel, (i % per_panel) // per_pair, i % per_pair, 0),
            ),
        ],
        out_specs=HBM,
        scratch_shapes=[pltpu.VMEM((count, length), F32), pltpu.SemaphoreType.DMA],
        compiler_params=pltpu.CompilerParams(vmem_limit_bytes=16 << 20),
    )(*[in_hbm(x) for x in solved], early, in_hbm(trail))
    flat = trail.reshape(panels, -1, 2 * rows, length)
    out, mine = call(
        lambda *refs: finish(panels - 1, *refs),
        [(length, count), (tail, count)],
        [HBM, HBM, HBM, SMEM, HBM, VMEM],
        [
            pltpu.VMEM((rows, count), F32),
            pltpu.VMEM(flat.shape[1:], F32),
            pltpu.VMEM(late.shape, F32),
            pltpu.VMEM(total.shape, F32),
            pltpu.VMEM((length, count), F32),
            pltpu.SemaphoreType.DMA((2 * flat.shape[1] + 2,)),
        ],
    )(in_hbm(late), in_hbm(flat), in_hbm(total), index, in_hbm(current), own)
    return (mine[None], out[None])


def solution(mesh):
    nx, ny, nz, nc = SIZES(mesh)
    fine = Mesh(
        mesh.devices.reshape(nx, QUADS, ny // QUADS, nz, nc), ("x", "yq", "yp", "z", "core")
    )
    row = ("x", "yq", "yp")
    in_specs = (P(row, None, None, RHS), P(row, None, RHS, None), P(row, None, RHS))
    out_specs = (P(row, None, RHS), P(row, None, RHS))
    return jax.shard_map(body, mesh=fine, in_specs=in_specs, out_specs=out_specs, check_vma=False)


def SIZES(mesh):
    nrow, nrhs = mesh.shape["row"], mesh.shape["rhs"]
    return nrow // 8, 8, nrhs // 2, 2
```

```python
import jax
import jax.numpy as jnp
from jax import lax
from jax.experimental import pallas as pl
from jax.experimental.pallas import tpu as pltpu
from jax.sharding import Mesh, PartitionSpec as P

QUADS = 4
RHS = ("z", "core")
GROUP = ("yp", "x")
F32 = jnp.float32


def halves(value):
    high = value.astype(jnp.bfloat16)
    return high, (value - high.astype(F32)).astype(jnp.bfloat16)


def dot(a, b, dims):
    def one(u, v):
        return lax.dot_general(u, v, (dims, ((), ())), preferred_element_type=F32)

    ah, al = halves(a)
    bh, bl = halves(b)
    return one(ah, bh) + (one(ah, bl) + one(al, bh))


NN = ((1,), (0,))
NT = ((1,), (1,))


VMEM = pl.BlockSpec(memory_space=pltpu.VMEM)
SMEM = pl.BlockSpec(memory_space=pltpu.SMEM)
HBM = pl.BlockSpec(memory_space=pltpu.HBM)


def call(kernel, shapes, in_specs, scratch=()):
    return pl.pallas_call(
        kernel,
        out_shape=[jax.ShapeDtypeStruct(s, F32) for s in shapes],
        in_specs=in_specs,
        out_specs=[VMEM] * len(shapes),
        scratch_shapes=scratch,
        compiler_params=pltpu.CompilerParams(vmem_limit_bytes=20 << 20),
    )


def in_hbm(array):
    return pltpu.with_memory_space_constraint(array, pltpu.HBM)


def whole(shape):
    return pl.BlockSpec(shape, lambda i: (0,) * len(shape))


def pack(f_hbm, inv_hbm, r_hbm, out_ref, f_ref, inv_ref, r_ref, sems):
    quads, _, lanes = out_ref.shape
    copies = [
        pltpu.make_async_copy(f_hbm.at[:, :, pl.ds(0, lanes)], f_ref, sems.at[0]),
        pltpu.make_async_copy(inv_hbm, inv_ref, sems.at[1]),
        pltpu.make_async_copy(r_hbm.at[pl.ds(0, lanes)], r_ref, sems.at[2]),
    ]
    for c in copies:
        c.start()
    for c in copies:
        c.wait()
    cols = f_ref.shape[1]
    per = r_ref.shape[1] // quads
    w = inv_ref.shape[1]
    turned = r_ref[...].T
    wide = jnp.concatenate([f_ref[0][:, w:], f_ref[2][:, 3 * w :]], axis=1)
    mid = f_ref[1][:, 2 * w :]
    mid = jnp.concatenate([mid[: cols // 2], mid[cols // 2 :]], axis=1)
    diag = jnp.concatenate([inv_ref[k].T for k in range(4)], axis=1)
    for q in range(quads):
        out_ref[q, :per] = turned[q * per : (q + 1) * per]
        out_ref[q, per : per + cols] = wide
        out_ref[q, per + cols : per + cols + cols // 2] = mid
        out_ref[q, per + cols + cols // 2 :] = diag


def sort(w, per, got_ref, heads_ref, pay_ref, first_ref):
    quads = got_ref.shape[0]
    half = pay_ref.shape[2]
    cols = 2 * half
    a, b, d = per, per + cols, per + cols + half

    def lanes(start, n, at):
        return jnp.concatenate(
            [got_ref[q, start : start + n][:, at : at + w] for q in range(quads)], axis=1
        )

    for k in range(4):
        heads_ref[k] = lanes(0, per, k * w)
    for h in range(2):
        for k in range(1, 4):
            pay_ref[k - 1, h] = lanes(d + h * half, half, k * w)
        for j in range(3):
            pay_ref[3 + j, h] = lanes(a + h * half, half, j * w)
        for j in range(2):
            pay_ref[6 + j, h] = lanes(b, half, h * 2 * w + j * w)
        pay_ref[8, h] = lanes(a + h * half, half, 3 * w)
        piece = lanes(d + h * half, half, 0)
        for c in range(first_ref.shape[0]):
            first_ref[c, h] = piece


def begin(core_ref, head_ref, mine_ref, other_ref, out_ref):
    n, pair, half, rows = mine_ref.shape
    head = head_ref[0]
    even = core_ref[0] == 0
    for p in range(pair):
        mine, other = mine_ref[:, p], other_ref[:, p]
        low = jnp.where(even, mine, other)
        high = jnp.where(even, other, mine)
        block = jnp.concatenate([low[:, None], high[:, None]], axis=1)
        y = dot(head, block.reshape(2 * n * half, rows), NT)
        m = 2 * n * half // rows
        for x in range(m):
            out_ref[p * m + x] = y[:, x * rows : (x + 1) * rows]


def add_all(got_ref, *refs):
    mine_refs, out_ref = refs[:-1], refs[-1]
    total = jnp.sum(got_ref[...], axis=0)
    for c in range(out_ref.shape[0]):
        for k, mine_ref in enumerate(mine_refs):
            out_ref[c, k] = mine_ref[...]
        out_ref[c, len(mine_refs)] = total


def add_up(got_ref, out_ref, mine_ref):
    total = jnp.sum(got_ref[...], axis=0)
    mine_ref[...] = total
    for c in range(out_ref.shape[0]):
        out_ref[c] = total


def advance(base, at, diag_at, solved_ref, head_ref, rest_hbm, y_out, line_ref, diag_ref, sems):
    group, rows = y_out.shape[0], y_out.shape[2]
    first = pltpu.make_async_copy(rest_hbm.at[at], line_ref, sems.at[0])
    second = pltpu.make_async_copy(rest_hbm.at[diag_at], diag_ref, sems.at[1])
    first.start()
    second.start()
    x = chosen(solved_ref)
    first.wait()
    head = head_ref[base] - dot(x, line_ref[...], NN)
    second.wait()
    y = dot(head, diag_ref[...], NT)
    for s in range(group):
        y_out[s] = y[:, s * rows : (s + 1) * rows]


def chosen(solved_ref):
    return jnp.concatenate([solved_ref[s] for s in range(solved_ref.shape[0])], axis=1)


def follow(base, at, solved_ref, heads_ref, rest_hbm, heads_out, lines_ref, sem):
    left = heads_out.shape[0]
    copy = pltpu.make_async_copy(rest_hbm.at[pl.ds(at, left)], lines_ref, sem)
    copy.start()
    x = chosen(solved_ref)
    copy.wait()
    for b in range(left):
        heads_out[b] = heads_ref[base + b + 1] - dot(x, lines_ref[b], NN)


def others(quad_ref, got_ref, out_ref):
    copies, panels, turns = out_ref.shape[:3]
    quads = got_ref.shape[0]
    for t in range(turns):
        q = lax.rem(quad_ref[0] + (t + 1), quads)
        for k in range(panels):
            block = got_ref[q, k]
            for c in range(copies):
                out_ref[c, k, t] = block


def last_copies(panel, got_ref, out_ref):
    for c in range(out_ref.shape[0]):
        for q in range(got_ref.shape[0]):
            out_ref[c, q] = got_ref[q, panel]


def trail_sum(steps, *refs):
    own_refs, (x_ref, f_ref, out_hbm, acc_ref, sem) = refs[:-5], refs[-5:]
    step = pl.program_id(0)

    @pl.when(step == 0)
    def _():
        acc_ref[...] = jnp.zeros_like(acc_ref)

    for k, own_ref in enumerate(own_refs):

        @pl.when(step // steps == k)
        def _():
            parts = []
            for s in range(x_ref.shape[0]):
                turns = [x_ref[s, 0, t] for t in range(x_ref.shape[2])]
                parts.append(jnp.concatenate([own_ref[x_ref.shape[0] * (step % steps) + s], *turns], axis=0))
            acc_ref[...] += dot(jnp.concatenate(parts, axis=1), f_ref[0, 0], NN)

    @pl.when(step == pl.num_programs(0) - 1)
    def _():
        copy = pltpu.make_async_copy(acc_ref, out_hbm, sem)
        copy.start()
        copy.wait()


def finish(panel, x_hbm, f_hbm, sum_hbm, quad_ref, r_hbm, own_ref, *refs):
    out_ref, mine_ref, turned_ref, f_ref, x_ref, sum_ref, r_ref, sems = refs
    n = f_ref.shape[0]
    quads, panels, per, _ = own_ref.shape
    width = mine_ref.shape[0] // panels
    copies = []
    for b in range(n):
        pair = pl.ds(2 * b, 2)
        copies += [
            pltpu.make_async_copy(x_hbm.at[pair], x_ref.at[pair], sems.at[2 * b]),
            pltpu.make_async_copy(f_hbm.at[panel, b], f_ref.at[b], sems.at[2 * b + 1]),
        ]
    sums = pltpu.make_async_copy(sum_hbm, sum_ref, sems.at[2 * n])
    rows = pltpu.make_async_copy(
        r_hbm.at[pl.ds(mine_ref.shape[0], r_ref.shape[0])], r_ref, sems.at[2 * n + 1]
    )
    for c in (*copies, sums, rows):
        c.start()
    quad = quad_ref[0]
    at = pl.multiple_of(quad * width, width)
    for k in range(panels):
        turned_ref[...] = jnp.concatenate([own_ref[q, k] for q in range(quads)], axis=0).T
        mine_ref[k * width : (k + 1) * width] = turned_ref[pl.ds(at, width)]
    total = None
    for b in range(n):
        copies[2 * b].wait()
        copies[2 * b + 1].wait()
        x = [x_ref[2 * b + s].reshape(-1, x_ref.shape[3]) for s in range(2)]
        product = dot(jnp.concatenate(x, axis=1), f_ref[b], NN)
        total = product if b == 0 else total + product
    sums.wait()
    total += jnp.concatenate(
        [
            sum_ref[pl.ds(pl.multiple_of(lax.rem(q + quads - quad, quads) * per, per), per)]
            for q in range(quads)
        ],
        axis=0,
    )
    rows.wait()
    out_ref[...] = r_ref[...] - total.T


def body(factor, inverses, right_side):
    lower = jnp.transpose(factor[0], (1, 2, 0))
    inv = jnp.transpose(inverses[0], (0, 2, 1))
    current = right_side[0]
    panels, cols, _ = lower.shape
    width = inv.shape[1]
    count = current.shape[1]
    tail = panels * width
    quads = lax.axis_size("yq")
    nx, npair = lax.axis_size("x"), lax.axis_size("yp")
    blocks = lax.axis_size(RHS)
    group = nx * npair
    per = count // quads
    rows = quads * width
    half = cols // npair
    quad = lax.axis_index("yq")

    index = quad.reshape(1).astype(jnp.int32)
    (sent,) = call(
        pack,
        [(quads, per + 2 * cols + half, tail)],
        [HBM, HBM, HBM],
        [
            pltpu.VMEM((panels, cols, tail), F32),
            pltpu.VMEM(inv.shape, F32),
            pltpu.VMEM((tail, count), F32),
            pltpu.SemaphoreType.DMA((3,)),
        ],
    )(in_hbm(lower), in_hbm(inv), in_hbm(current))
    got = lax.all_to_all(sent, "yq", 0, 0, tiled=True)
    trail = lower[:, :, tail:].reshape(panels, npair, half, -1)
    core = lax.axis_index("core").reshape(1).astype(jnp.int32)
    got, trail, index, core = lax.optimization_barrier((got, trail, index, core))
    heads, pay, first = call(
        lambda *refs: sort(width, per, *refs),
        [(panels, per, rows), (9, npair, half, rows), (blocks // 2, npair, half, rows)],
        [VMEM],
    )(got)
    first = lax.all_to_all(first, "z", 0, 0, tiled=True)
    other = lax.ppermute(first, "core", [(0, 1), (1, 0)])
    rest = lax.all_gather(pay, RHS, axis=2, tiled=True)
    trail = lax.all_gather(trail, RHS, axis=2, tiled=True)
    rest = rest.reshape(9, group * rows, rows)

    (y,) = call(begin, [(group, per, rows)], [SMEM, VMEM, VMEM, VMEM])(core, heads, first, other)
    length = lower.shape[2] - tail
    mine, solved = [], []
    for k in range(panels):
        got = lax.all_to_all(y, GROUP, 0, 0, tiled=True)
        if k == panels - 1:
            break
        copied, single = call(add_up, [(group, per, rows), (per, rows)], [VMEM])(got)
        mine.append(single)
        solved.append(lax.all_to_all(copied, GROUP, 0, 0, tiled=True))
        left = panels - 1 - k
        at = {3: 3, 2: 6, 1: 8}[left]
        one = pltpu.VMEM((group * rows, rows), F32)
        (y,) = call(
            lambda *refs, at=at, k=k: advance(int(k == 0), at, k, *refs),
            [(group, per, rows)],
            [VMEM, VMEM, HBM],
            [one, one, pltpu.SemaphoreType.DMA((2,))],
        )(solved[k], heads, in_hbm(rest))
        if left > 1:
            (heads,) = call(
                lambda *refs, at=at, k=k: follow(int(k == 0), at + 1, *refs),
                [(left - 1, per, rows)],
                [VMEM, VMEM, HBM],
                [
                    pltpu.VMEM((left - 1, group * rows, rows), F32),
                    pltpu.SemaphoreType.DMA,
                ],
            )(solved[k], heads, in_hbm(rest))

    (sent,) = call(add_all, [(quads, panels, per, rows)], [VMEM] * panels)(got, *mine)
    own = lax.all_to_all(sent, "yq", 0, 0, tiled=True)
    (sent,) = call(others, [(group, panels - 1, quads - 1, per, rows)], [SMEM, VMEM])(index, own)
    early = lax.all_to_all(sent, GROUP, 0, 0, tiled=True)
    own, early = lax.optimization_barrier((own, early))
    (sent,) = call(lambda *refs: last_copies(panels - 1, *refs), [(group, quads, per, rows)], [VMEM])(own)
    late = lax.all_to_all(sent, GROUP, 0, 0, tiled=True)

    per_panel = npair
    total = pl.pallas_call(
        lambda *refs: trail_sum(per_panel, *refs),
        out_shape=pltpu.HBM((count, length), F32),
        grid=((panels - 1) * per_panel,),
        in_specs=[
            *[whole((group, per, rows))] * (panels - 1),
            pl.BlockSpec(
                (nx, 1, quads - 1, per, rows), lambda i: (i % per_panel, i // per_panel, 0, 0, 0)
            ),
            pl.BlockSpec(
                (1, 1, nx * rows, length), lambda i: (i // per_panel, i % per_panel, 0, 0)
            ),
        ],
        out_specs=HBM,
        scratch_shapes=[pltpu.VMEM((count, length), F32), pltpu.SemaphoreType.DMA],
        compiler_params=pltpu.CompilerParams(vmem_limit_bytes=24 << 20),
    )(*[in_hbm(x) for x in solved], early, in_hbm(trail))
    flat = trail.reshape(panels, -1, 2 * rows, length)
    out, mine = call(
        lambda *refs: finish(panels - 1, *refs),
        [(length, count), (tail, count)],
        [HBM, HBM, HBM, SMEM, HBM, VMEM],
        [
            pltpu.VMEM((rows, count), F32),
            pltpu.VMEM(flat.shape[1:], F32),
            pltpu.VMEM(late.shape, F32),
            pltpu.VMEM(total.shape, F32),
            pltpu.VMEM((length, count), F32),
            pltpu.SemaphoreType.DMA((2 * flat.shape[1] + 2,)),
        ],
    )(in_hbm(late), in_hbm(flat), in_hbm(total), index, in_hbm(current), own)
    return (mine[None], out[None])


def solution(mesh):
    nx, ny, nz, nc = SIZES(mesh)
    fine = Mesh(
        mesh.devices.reshape(nx, QUADS, ny // QUADS, nz, nc), ("x", "yq", "yp", "z", "core")
    )
    row = ("x", "yq", "yp")
    in_specs = (P(row, None, None, RHS), P(row, None, RHS, None), P(row, None, RHS))
    out_specs = (P(row, None, RHS), P(row, None, RHS))
    return jax.shard_map(body, mesh=fine, in_specs=in_specs, out_specs=out_specs, check_vma=False)


def SIZES(mesh):
    nrow, nrhs = mesh.shape["row"], mesh.shape["rhs"]
    return nrow // 8, 8, nrhs // 2, 2
```

```python
import jax
import jax.numpy as jnp
from jax import lax
from jax.experimental import pallas as pl
from jax.experimental.pallas import tpu as pltpu
from jax.sharding import Mesh, PartitionSpec as P

QUADS = 4
RHS = ("z", "core")
GROUP = ("yp", "x")
F32 = jnp.float32


def halves(value):
    high = value.astype(jnp.bfloat16)
    return high, (value - high.astype(F32)).astype(jnp.bfloat16)


def dot(a, b, dims):
    def one(u, v):
        return lax.dot_general(u, v, (dims, ((), ())), preferred_element_type=F32)

    ah, al = halves(a)
    bh, bl = halves(b)
    return one(ah, bh) + (one(ah, bl) + one(al, bh))


NN = ((1,), (0,))
NT = ((1,), (1,))


VMEM = pl.BlockSpec(memory_space=pltpu.VMEM)
SMEM = pl.BlockSpec(memory_space=pltpu.SMEM)
HBM = pl.BlockSpec(memory_space=pltpu.HBM)


def call(kernel, shapes, in_specs, scratch=()):
    return pl.pallas_call(
        kernel,
        out_shape=[jax.ShapeDtypeStruct(s, F32) for s in shapes],
        in_specs=in_specs,
        out_specs=[VMEM] * len(shapes),
        scratch_shapes=scratch,
        compiler_params=pltpu.CompilerParams(vmem_limit_bytes=20 << 20),
    )


def in_hbm(array):
    return pltpu.with_memory_space_constraint(array, pltpu.HBM)


def whole(shape):
    return pl.BlockSpec(shape, lambda i: (0,) * len(shape))


def pack(f_hbm, inv_hbm, r_hbm, out_ref, f_ref, inv_ref, r_ref, sems):
    quads, _, lanes = out_ref.shape
    copies = [
        pltpu.make_async_copy(f_hbm.at[:, :, pl.ds(0, lanes)], f_ref, sems.at[0]),
        pltpu.make_async_copy(inv_hbm, inv_ref, sems.at[1]),
        pltpu.make_async_copy(r_hbm.at[pl.ds(0, lanes)], r_ref, sems.at[2]),
    ]
    for c in copies:
        c.start()
    for c in copies:
        c.wait()
    cols = f_ref.shape[1]
    per = r_ref.shape[1] // quads
    w = inv_ref.shape[1]
    turned = r_ref[...].T
    wide = jnp.concatenate([f_ref[0][:, w:], f_ref[2][:, 3 * w :]], axis=1)
    mid = f_ref[1][:, 2 * w :]
    mid = jnp.concatenate([mid[: cols // 2], mid[cols // 2 :]], axis=1)
    diag = jnp.concatenate([inv_ref[k].T for k in range(4)], axis=1)
    for q in range(quads):
        out_ref[q, :per] = turned[q * per : (q + 1) * per]
        out_ref[q, per : per + cols] = wide
        out_ref[q, per + cols : per + cols + cols // 2] = mid
        out_ref[q, per + cols + cols // 2 :] = diag


def sort(w, per, got_ref, heads_ref, pay_ref, first_ref):
    quads = got_ref.shape[0]
    half = pay_ref.shape[2]
    cols = 2 * half
    a, b, d = per, per + cols, per + cols + half

    def lanes(start, n, at):
        return jnp.concatenate(
            [got_ref[q, start : start + n][:, at : at + w] for q in range(quads)], axis=1
        )

    for k in range(4):
        heads_ref[k] = lanes(0, per, k * w)
    for h in range(2):
        for k in range(1, 4):
            pay_ref[k - 1, h] = lanes(d + h * half, half, k * w)
        for j in range(3):
            pay_ref[3 + j, h] = lanes(a + h * half, half, j * w)
        for j in range(2):
            pay_ref[6 + j, h] = lanes(b, half, h * 2 * w + j * w)
        pay_ref[8, h] = lanes(a + h * half, half, 3 * w)
        piece = lanes(d + h * half, half, 0)
        for c in range(first_ref.shape[0]):
            first_ref[c, h] = piece


def begin(core_ref, head_ref, mine_ref, other_ref, out_ref):
    n, pair, half, rows = mine_ref.shape
    head = head_ref[0]
    even = core_ref[0] == 0
    for p in range(pair):
        mine, other = mine_ref[:, p], other_ref[:, p]
        low = jnp.where(even, mine, other)
        high = jnp.where(even, other, mine)
        block = jnp.concatenate([low[:, None], high[:, None]], axis=1)
        y = dot(head, block.reshape(2 * n * half, rows), NT)
        m = 2 * n * half // rows
        for x in range(m):
            out_ref[p * m + x] = y[:, x * rows : (x + 1) * rows]


def add_all(got_ref, *refs):
    mine_refs, out_ref = refs[:-1], refs[-1]
    total = jnp.sum(got_ref[...], axis=0)
    for c in range(out_ref.shape[0]):
        for k, mine_ref in enumerate(mine_refs):
            out_ref[c, k] = mine_ref[...]
        out_ref[c, len(mine_refs)] = total


def add_up(got_ref, out_ref, mine_ref):
    total = jnp.sum(got_ref[...], axis=0)
    mine_ref[...] = total
    for c in range(out_ref.shape[0]):
        out_ref[c] = total


def advance(base, at, diag_at, solved_ref, head_ref, rest_hbm, y_out, line_ref, diag_ref, sems):
    group, rows = y_out.shape[0], y_out.shape[2]
    first = pltpu.make_async_copy(rest_hbm.at[at], line_ref, sems.at[0])
    second = pltpu.make_async_copy(rest_hbm.at[diag_at], diag_ref, sems.at[1])
    first.start()
    second.start()
    x = chosen(solved_ref)
    first.wait()
    head = head_ref[base] - dot(x, line_ref[...], NN)
    second.wait()
    y = dot(head, diag_ref[...], NT)
    for s in range(group):
        y_out[s] = y[:, s * rows : (s + 1) * rows]


def chosen(solved_ref):
    return jnp.concatenate([solved_ref[s] for s in range(solved_ref.shape[0])], axis=1)


def follow(base, at, solved_ref, heads_ref, rest_hbm, heads_out, lines_ref, sem):
    left = heads_out.shape[0]
    copy = pltpu.make_async_copy(rest_hbm.at[pl.ds(at, left)], lines_ref, sem)
    copy.start()
    x = chosen(solved_ref)
    copy.wait()
    for b in range(left):
        heads_out[b] = heads_ref[base + b + 1] - dot(x, lines_ref[b], NN)


def others(quad_ref, got_ref, out_ref):
    copies, panels, turns = out_ref.shape[:3]
    quads = got_ref.shape[0]
    for t in range(turns):
        q = lax.rem(quad_ref[0] + (t + 1), quads)
        for k in range(panels):
            block = got_ref[q, k]
            for c in range(copies):
                out_ref[c, k, t] = block


def last_copies(panel, got_ref, out_ref):
    for c in range(out_ref.shape[0]):
        for q in range(got_ref.shape[0]):
            out_ref[c, q] = got_ref[q, panel]


def trail_sum(steps, *refs):
    own_refs, (x_ref, f_ref, quad_ref, r_ref, out_hbm, acc_ref, turned_ref, sem) = (
        refs[:-8],
        refs[-8:],
    )
    step = pl.program_id(0)

    @pl.when(step == 0)
    def _():
        turned_ref[...] = r_ref[r_ref.shape[0] - turned_ref.shape[1] :].T
        quads, per = x_ref.shape[2] + 1, x_ref.shape[3]
        for t in range(quads):
            q = lax.rem(quad_ref[0] + t, quads)
            acc_ref[t * per : (t + 1) * per] = turned_ref[
                pl.ds(pl.multiple_of(q * per, per), per)
            ]

    for k, own_ref in enumerate(own_refs):

        @pl.when(step // steps == k)
        def _():
            parts = []
            for s in range(x_ref.shape[0]):
                turns = [x_ref[s, 0, t] for t in range(x_ref.shape[2])]
                parts.append(jnp.concatenate([own_ref[x_ref.shape[0] * (step % steps) + s], *turns], axis=0))
            acc_ref[...] -= dot(jnp.concatenate(parts, axis=1), f_ref[0, 0], NN)

    @pl.when(step == pl.num_programs(0) - 1)
    def _():
        copy = pltpu.make_async_copy(acc_ref, out_hbm, sem)
        copy.start()
        copy.wait()


def finish(panel, x_hbm, f_hbm, sum_hbm, quad_ref, own_ref, *refs):
    out_ref, mine_ref, turned_ref, f_ref, x_ref, sum_ref, sems = refs
    n = f_ref.shape[0]
    quads, panels, per, _ = own_ref.shape
    width = mine_ref.shape[0] // panels
    copies = []
    for b in range(n):
        pair = pl.ds(2 * b, 2)
        copies += [
            pltpu.make_async_copy(x_hbm.at[pair], x_ref.at[pair], sems.at[2 * b]),
            pltpu.make_async_copy(f_hbm.at[panel, b], f_ref.at[b], sems.at[2 * b + 1]),
        ]
    sums = pltpu.make_async_copy(sum_hbm, sum_ref, sems.at[2 * n])
    for c in (*copies, sums):
        c.start()
    quad = quad_ref[0]
    at = pl.multiple_of(quad * width, width)
    for k in range(panels):
        turned_ref[...] = jnp.concatenate([own_ref[q, k] for q in range(quads)], axis=0).T
        mine_ref[k * width : (k + 1) * width] = turned_ref[pl.ds(at, width)]
    total = None
    for b in range(n):
        copies[2 * b].wait()
        copies[2 * b + 1].wait()
        x = [x_ref[2 * b + s].reshape(-1, x_ref.shape[3]) for s in range(2)]
        product = dot(jnp.concatenate(x, axis=1), f_ref[b], NN)
        total = product if b == 0 else total + product
    sums.wait()
    left = jnp.concatenate(
        [
            sum_ref[pl.ds(pl.multiple_of(lax.rem(q + quads - quad, quads) * per, per), per)]
            for q in range(quads)
        ],
        axis=0,
    )
    out_ref[...] = (left - total).T


def body(factor, inverses, right_side):
    lower = jnp.transpose(factor[0], (1, 2, 0))
    inv = jnp.transpose(inverses[0], (0, 2, 1))
    current = right_side[0]
    panels, cols, _ = lower.shape
    width = inv.shape[1]
    count = current.shape[1]
    tail = panels * width
    quads = lax.axis_size("yq")
    nx, npair = lax.axis_size("x"), lax.axis_size("yp")
    blocks = lax.axis_size(RHS)
    group = nx * npair
    per = count // quads
    rows = quads * width
    half = cols // npair
    quad = lax.axis_index("yq")

    index = quad.reshape(1).astype(jnp.int32)
    (sent,) = call(
        pack,
        [(quads, per + 2 * cols + half, tail)],
        [HBM, HBM, HBM],
        [
            pltpu.VMEM((panels, cols, tail), F32),
            pltpu.VMEM(inv.shape, F32),
            pltpu.VMEM((tail, count), F32),
            pltpu.SemaphoreType.DMA((3,)),
        ],
    )(in_hbm(lower), in_hbm(inv), in_hbm(current))
    got = lax.all_to_all(sent, "yq", 0, 0, tiled=True)
    trail = lower[:, :, tail:].reshape(panels, npair, half, -1)
    core = lax.axis_index("core").reshape(1).astype(jnp.int32)
    got, trail, index, core = lax.optimization_barrier((got, trail, index, core))
    heads, pay, first = call(
        lambda *refs: sort(width, per, *refs),
        [(panels, per, rows), (9, npair, half, rows), (blocks // 2, npair, half, rows)],
        [VMEM],
    )(got)
    first = lax.all_to_all(first, "z", 0, 0, tiled=True)
    other = lax.ppermute(first, "core", [(0, 1), (1, 0)])
    rest = lax.all_gather(pay, RHS, axis=2, tiled=True)
    trail = lax.all_gather(trail, RHS, axis=2, tiled=True)
    rest = rest.reshape(9, group * rows, rows)

    (y,) = call(begin, [(group, per, rows)], [SMEM, VMEM, VMEM, VMEM])(core, heads, first, other)
    length = lower.shape[2] - tail
    mine, solved = [], []
    for k in range(panels):
        got = lax.all_to_all(y, GROUP, 0, 0, tiled=True)
        if k == panels - 1:
            break
        copied, single = call(add_up, [(group, per, rows), (per, rows)], [VMEM])(got)
        mine.append(single)
        solved.append(lax.all_to_all(copied, GROUP, 0, 0, tiled=True))
        left = panels - 1 - k
        at = {3: 3, 2: 6, 1: 8}[left]
        one = pltpu.VMEM((group * rows, rows), F32)
        (y,) = call(
            lambda *refs, at=at, k=k: advance(int(k == 0), at, k, *refs),
            [(group, per, rows)],
            [VMEM, VMEM, HBM],
            [one, one, pltpu.SemaphoreType.DMA((2,))],
        )(solved[k], heads, in_hbm(rest))
        if left > 1:
            (heads,) = call(
                lambda *refs, at=at, k=k: follow(int(k == 0), at + 1, *refs),
                [(left - 1, per, rows)],
                [VMEM, VMEM, HBM],
                [
                    pltpu.VMEM((left - 1, group * rows, rows), F32),
                    pltpu.SemaphoreType.DMA,
                ],
            )(solved[k], heads, in_hbm(rest))

    (sent,) = call(add_all, [(quads, panels, per, rows)], [VMEM] * panels)(got, *mine)
    own = lax.all_to_all(sent, "yq", 0, 0, tiled=True)
    (sent,) = call(others, [(group, panels - 1, quads - 1, per, rows)], [SMEM, VMEM])(index, own)
    early = lax.all_to_all(sent, GROUP, 0, 0, tiled=True)
    own, early = lax.optimization_barrier((own, early))
    (sent,) = call(lambda *refs: last_copies(panels - 1, *refs), [(group, quads, per, rows)], [VMEM])(own)
    late = lax.all_to_all(sent, GROUP, 0, 0, tiled=True)

    per_panel = npair
    total = pl.pallas_call(
        lambda *refs: trail_sum(per_panel, *refs),
        out_shape=pltpu.HBM((count, length), F32),
        grid=((panels - 1) * per_panel,),
        in_specs=[
            *[whole((group, per, rows))] * (panels - 1),
            pl.BlockSpec(
                (nx, 1, quads - 1, per, rows), lambda i: (i % per_panel, i // per_panel, 0, 0, 0)
            ),
            pl.BlockSpec(
                (1, 1, nx * rows, length), lambda i: (i // per_panel, i % per_panel, 0, 0)
            ),
            SMEM,
            whole(current.shape),
        ],
        out_specs=HBM,
        scratch_shapes=[pltpu.VMEM((count, length), F32)] * 2 + [pltpu.SemaphoreType.DMA],
        compiler_params=pltpu.CompilerParams(vmem_limit_bytes=24 << 20),
    )(*[in_hbm(x) for x in solved], early, in_hbm(trail), index, in_hbm(current))
    flat = trail.reshape(panels, -1, 2 * rows, length)
    out, mine = call(
        lambda *refs: finish(panels - 1, *refs),
        [(length, count), (tail, count)],
        [HBM, HBM, HBM, SMEM, VMEM],
        [
            pltpu.VMEM((rows, count), F32),
            pltpu.VMEM(flat.shape[1:], F32),
            pltpu.VMEM(late.shape, F32),
            pltpu.VMEM(total.shape, F32),
            pltpu.SemaphoreType.DMA((2 * flat.shape[1] + 1,)),
        ],
    )(in_hbm(late), in_hbm(flat), in_hbm(total), index, own)
    return (mine[None], out[None])


def solution(mesh):
    nx, ny, nz, nc = SIZES(mesh)
    fine = Mesh(
        mesh.devices.reshape(nx, QUADS, ny // QUADS, nz, nc), ("x", "yq", "yp", "z", "core")
    )
    row = ("x", "yq", "yp")
    in_specs = (P(row, None, None, RHS), P(row, None, RHS, None), P(row, None, RHS))
    out_specs = (P(row, None, RHS), P(row, None, RHS))
    return jax.shard_map(body, mesh=fine, in_specs=in_specs, out_specs=out_specs, check_vma=False)


def SIZES(mesh):
    nrow, nrhs = mesh.shape["row"], mesh.shape["rhs"]
    return nrow // 8, 8, nrhs // 2, 2
```
